32 devices in a mesh: gx: 4 (over y, x), gy: 8 (over z, core).
Axes of the slice: x: 2, y: 2, z: 4, core: 2. Of those that a mesh axis runs over, the one named last changes fastest.
Arguments:
- chemical_concentration: float32 [53, 128, 1024], P(None, 'gx', 'gy'), may hold values from 0.01 to 1
- thermal_scaled: float32 [128, 1024], P('gx', 'gy'), may hold values from 1 to 2.5
- tentative_flow_spread: float32 [128, 1024], P('gx', 'gy'), may hold values from -6 to 6
- substep_numbers: int32 [4, 32], P('gx', 'gy'), may hold values from 1 to 4, as said below
- patch_holder_lookup: int32 [4, 32], P('gx', 'gy'), may hold values from 0 to 3, as said below
- consumed_weighting: float32 [325, 53], replicated, may hold values from -0.875 to 0.875
- molar_coefficient: float32 [325, 53], replicated, may hold values from -0.15625 to 0.15625
- frequency_factor_log: float32 [325], replicated, may hold values from -1 to 1
- arrhenius_energy: float32 [325], replicated, may hold values from 0.5 to 3
- enthalpy_released: float32 [325], replicated, may hold values from -0.3125 to 0.3125
Outputs:
- chemicals_after_window: float32 [53, 128, 1024], P(None, 'gx', 'gy')
- thermal_after_window: float32 [128, 1024], P('gx', 'gy')
- scalar_potential_field: float32 [128, 1024], P('gx', 'gy')
- holder_energy_burden: float32 [4, 8], P('gx', 'gy')
The draws below stay inside these ranges and needn't reach their ends.
Inputs may be any that keep to these rules, and one draw needn't show every extreme that they name: `substep_numbers`: every block has 4 on some tile. `patch_holder_lookup`: in each block's 4 entries every owner 0 to 3 appears exactly 1 times.
All inputs are finite; a program needn't handle non-finite values.
Results may differ from the reference program's by a relative error of at most 0.0003.
Values sent between devices are 32-bit elements; how exact they have to be, the bound alone decides.
No kernel may reach another device: no remote copies, remote signals or barrier semaphores. Data moves between devices by JAX's collectives and lax.ppermute only.
A program may use at most 64 MiB of HBM per device.

```python
import math
import jax
import jax.numpy as jnp
from jax import lax

NS = 53
NR = 325
CHIP_SPAN_ALPHA = 32
CHIP_SPAN_BETA = 128
MAXSUB = 4
LEVELS = 3
SWEEPS = 2
COARSE = 4
CHIP_PATCHES = 4
PATCH_VOLUMES = 1024
MESH_SPAN_ALPHA = 128
MESH_SPAN_BETA = 1024
N_GX = 4
N_GY = 8


def tile_counts(key):
    heavy_key = jax.random.fold_in(key, 11)
    raw_key = jax.random.fold_in(key, 12)
    heaviness = jax.random.randint(heavy_key, (N_GX, N_GY, 1), 0, MAXSUB)
    raw = jax.random.randint(raw_key, (N_GX, N_GY, CHIP_PATCHES), 0, MAXSUB - 1)
    tallies = jnp.where(raw < heaviness, MAXSUB, 1)
    tallies = tallies.at[:, :, 0].set(MAXSUB)
    return tallies.astype(jnp.int32)


def draw_substep_numbers(key, part):
    tallies = tile_counts(key)
    return tallies.reshape(N_GX, N_GY * CHIP_PATCHES).astype(jnp.int32)


def draw_patch_holder_lookup(key, part):
    tallies = tile_counts(key)
    base = jax.random.fold_in(key, 21)
    keys = jax.random.split(base, N_GX * N_GY)
    breaker = jax.vmap(lambda single: jax.random.permutation(single, CHIP_PATCHES))(keys)
    breaker = breaker.reshape(N_GX, N_GY, CHIP_PATCHES).astype(jnp.int32)
    score = tallies * CHIP_PATCHES + breaker
    order = jnp.argsort(-score, axis=-1, stable=True)
    ranks = jnp.argsort(order, axis=-1, stable=True).astype(jnp.int32)
    row_index = jnp.arange(N_GX, dtype=jnp.int32)[:, None, None]
    owners = (ranks + row_index) % N_GX
    return owners.reshape(N_GX, N_GY * CHIP_PATCHES).astype(jnp.int32)


def steps_of(key, shape, cuts, low, top_value):
    gain = 1.0
    for dim, blocks in cuts:
        heights = jax.random.uniform(jax.random.fold_in(jax.random.fold_in(key, 6), dim), (blocks,), jnp.float32, low / len(cuts), top_value / len(cuts))
        gain = gain * jnp.repeat(jnp.exp(heights), shape[dim] // blocks).reshape((-1,) + (1,) * (len(shape) - 1 - dim))
    return gain


def scatter_about(stream_key, dims, spread, most, pieces=(), kind=jnp.bfloat16):
    array = jax.random.normal(stream_key, dims, jnp.float32) * spread
    if len(pieces) > 0:
        array = steps_of(stream_key, dims, pieces, -0.22, 0.18) * array
    return jnp.clip(array, min=-most, max=most).astype(kind)


def setup_inputs(seed: int = 0) -> dict:
    streams_of = jax.random.split(jax.random.key(seed), 11)
    return {
        "chemical_concentration": jnp.clip(jnp.exp(math.log(1.0) - 4.6051702 * jax.random.uniform(streams_of[0], (NS, MESH_SPAN_ALPHA, MESH_SPAN_BETA), jnp.float32) ** steps_of(streams_of[0], (NS, MESH_SPAN_ALPHA, MESH_SPAN_BETA), ((1, 4), (2, 8)), -0.2, 0.2)), 0.01, 1.0),
        "thermal_scaled": jnp.clip(1.0 + 1.5 * jax.random.uniform(streams_of[1], (MESH_SPAN_ALPHA, MESH_SPAN_BETA), jnp.float32) ** steps_of(streams_of[1], (MESH_SPAN_ALPHA, MESH_SPAN_BETA), ((0, 4), (1, 8)), -0.2, 0.2), 1.0, 2.5),
        "tentative_flow_spread": scatter_about(streams_of[2], (MESH_SPAN_ALPHA, MESH_SPAN_BETA), 1.0, 6.0, ((0, 4), (1, 8)), jnp.float32),
        "substep_numbers": draw_substep_numbers(jax.random.fold_in(streams_of[10], 71), 0),
        "patch_holder_lookup": draw_patch_holder_lookup(jax.random.fold_in(streams_of[10], 71), 0),
        "consumed_weighting": scatter_about(streams_of[5], (NR, NS), NS ** -0.5, 0.875, (), jnp.float32),
        "molar_coefficient": scatter_about(streams_of[6], (NR, NS), (4 * NR) ** -0.5, 0.15625, (), jnp.float32),
        "frequency_factor_log": jnp.clip(jax.random.uniform(streams_of[7], (NR,), jnp.float32, -1.0, 1.0), -1.0, 1.0),
        "arrhenius_energy": jnp.clip(jax.random.uniform(streams_of[8], (NR,), jnp.float32, 0.5, 3.0), 0.5, 3.0),
        "enthalpy_released": scatter_about(streams_of[9], (NR,), NR ** -0.5, 0.3125, (), jnp.float32),
    }


step_time = 0.4
relax = 0.8
high = lax.Precision.HIGHEST


def advance_chemistry(spec_in, temp_in, tallies, consumed_weighting, molar_coefficient, frequency_factor_log, arrhenius_energy, enthalpy_released, bound):
    width = step_time / tallies.astype(jnp.float32)
    heat_in = jnp.zeros_like(temp_in)

    def sweep(turn, carry):
        spec_now, temp_now, heat_now = carry
        delta = jnp.where(turn < tallies, width, 0.0)
        progress = jnp.einsum('rs,sbc->rbc', consumed_weighting, spec_now, precision=high)
        rates = jnp.exp(frequency_factor_log[:, None, None] - arrhenius_energy[:, None, None] / (1.0 + jnp.abs(temp_now))[None])
        flux = rates * progress
        change = jnp.einsum('rs,rbc->sbc', molar_coefficient, flux, precision=high)
        release = jnp.einsum('r,rbc->bc', enthalpy_released, flux, precision=high)
        return (spec_now + delta[None, :, None] * change, temp_now + delta[:, None] * release, heat_now + delta[:, None] * release)

    return lax.fori_loop(0, bound, sweep, (spec_in, temp_in, heat_in))


def gather_patches(grid):
    lead = grid.shape[:-2]
    depth = len(lead)
    split = grid.reshape(lead + (N_GX, CHIP_SPAN_ALPHA, N_GY, CHIP_SPAN_BETA))
    split = jnp.moveaxis(split, (depth, depth + 2), (0, 1))
    return split.reshape((N_GX * N_GY,) + lead + (CHIP_SPAN_ALPHA * CHIP_SPAN_BETA,))


def scatter_patches(blocks, lead):
    depth = len(lead)
    joined = blocks.reshape((N_GX, N_GY) + lead + (CHIP_SPAN_ALPHA, CHIP_SPAN_BETA))
    joined = jnp.moveaxis(joined, (0, 1), (depth, depth + 2))
    return joined.reshape(lead + (N_GX * CHIP_SPAN_ALPHA, N_GY * CHIP_SPAN_BETA))


def beside_all(field):
    padded = jnp.pad(field, 1)
    return padded[2:, 1:-1] + padded[:-2, 1:-1] + padded[1:-1, 2:] + padded[1:-1, :-2]


def smooth(field, rhs, scale):
    return field + relax * (scale * rhs - 4.0 * field + beside_all(field)) / 4.0


def vcycle(rhs, level):
    scale = 4.0 ** level
    field = jnp.zeros_like(rhs)
    if level == LEVELS - 1:
        for turn in range(COARSE):
            field = smooth(field, rhs, scale)
        return field
    for turn in range(SWEEPS):
        field = smooth(field, rhs, scale)
    resid = rhs - (4.0 * field - beside_all(field)) / scale
    leading_span, trailing_span = resid.shape
    coarse = resid.reshape(leading_span // 2, 2, trailing_span // 2, 2).mean(axis=(1, 3))
    correction = vcycle(coarse, level + 1)
    field = field + jnp.repeat(jnp.repeat(correction, 2, axis=0), 2, axis=1)
    for turn in range(SWEEPS):
        field = smooth(field, rhs, scale)
    return field


def reference(chemical_concentration, thermal_scaled, tentative_flow_spread, substep_numbers, patch_holder_lookup, consumed_weighting, molar_coefficient, frequency_factor_log, arrhenius_energy, enthalpy_released):
    chip_total = N_GX * N_GY
    chemical_patches = gather_patches(chemical_concentration).reshape(chip_total, NS, CHIP_PATCHES, PATCH_VOLUMES)
    thermal_patches = gather_patches(thermal_scaled).reshape(chip_total, CHIP_PATCHES, PATCH_VOLUMES)
    tallies = substep_numbers.reshape(N_GX, N_GY, CHIP_PATCHES).reshape(chip_total, CHIP_PATCHES)

    def single_patch(packed):
        spec_one, temp_one, count_one = packed
        return advance_chemistry(spec_one, temp_one, count_one, consumed_weighting, molar_coefficient, frequency_factor_log, arrhenius_energy, enthalpy_released, MAXSUB)

    updated_chemicals, thermal_following, thermal_release = lax.map(single_patch, (chemical_patches, thermal_patches, tallies))
    tile_sums = jnp.sum(thermal_release * thermal_release, axis=-1).reshape(N_GX, N_GY, CHIP_PATCHES)
    owners = patch_holder_lookup.reshape(N_GX, N_GY, CHIP_PATCHES)
    onehot = (owners[..., None] == jnp.arange(N_GX, dtype=jnp.int32)).astype(jnp.float32)
    holder_energy_burden = jnp.einsum('xyt,xyto->oy', tile_sums, onehot, precision=high) / (CHIP_SPAN_ALPHA * CHIP_SPAN_BETA)
    chemicals_after_window = scatter_patches(updated_chemicals.reshape(chip_total, NS, CHIP_SPAN_ALPHA * CHIP_SPAN_BETA), (NS,))
    thermal_after_window = scatter_patches(thermal_following.reshape(chip_total, CHIP_SPAN_ALPHA * CHIP_SPAN_BETA), ())
    heat_grid = scatter_patches(thermal_release.reshape(chip_total, CHIP_SPAN_ALPHA * CHIP_SPAN_BETA), ())
    scalar_potential_field = vcycle(tentative_flow_spread + heat_grid, 0)
    return chemicals_after_window, thermal_after_window, scalar_potential_field, holder_energy_burden
```

```python
import functools
import math

import jax
import jax.numpy as jnp
from jax import lax
from jax.experimental import pallas as pl
from jax.experimental.pallas import tpu as pltpu
from jax.sharding import PartitionSpec as P

LEVELS = 3
SWEEPS = 2
COARSE = 4

step_time = 0.4
relax = 0.8
lanes = 128
log2e = math.log2(math.e)
f32 = jnp.float32
bf16 = jnp.bfloat16
high = lax.Precision.HIGHEST


def round_up(value, multiple):
    return -(-value // multiple) * multiple


def halves(value):
    top = value.astype(bf16)
    return top, (value - top.astype(f32)).astype(bf16)


def chemistry_kernel(
    tallies,
    owners,
    spec_ref,
    temp_ref,
    flow_ref,
    consumed_ref,
    molar_ref,
    factor_ref,
    energy_ref,
    enthalpy_ref,
    spec_out,
    temp_out,
    rhs_out,
    share_out,
    state,
    gather_w,
    scatter_hi,
    scatter_lo,
    factor_b,
    energy_b,
    staging,
    *,
    tiles,
):
    species, rows, width = spec_ref.shape
    reactions = consumed_ref.shape[0]
    depth = state.shape[1]
    pad_r = gather_w.shape[0]
    tile_rows = rows // tiles
    tile_len = tile_rows * width

    staging[...] = jnp.zeros_like(staging)
    staging[:reactions, :species] = consumed_ref[...]
    top, low = halves(staging[:pad_r, :depth])
    gather_w[...] = jnp.concatenate([top, top, low], axis=1)
    staging[:reactions, :species] = molar_ref[...]
    turned = jnp.transpose(staging[...])
    row = lax.broadcasted_iota(jnp.int32, (depth, staging.shape[0]), 0)
    turned = turned[:depth]
    enthalpy = jnp.pad(enthalpy_ref[...], ((0, 0), (0, staging.shape[0] - reactions)))
    turned = jnp.where((row == species) | (row == species + 1), enthalpy, turned)
    top, low = halves(turned[:, :pad_r])
    scatter_hi[...] = jnp.concatenate([top, low], axis=0)
    scatter_lo[...] = top
    both = jnp.concatenate([factor_ref[...], energy_ref[...]], axis=0) * log2e
    both = jnp.pad(both, ((0, 6), (0, staging.shape[0] - reactions)))
    both = jnp.concatenate([both, jnp.zeros((lanes - 8, staging.shape[0]), f32)], axis=0)
    columns = jnp.transpose(both)
    factor_b[...] = jnp.broadcast_to(columns[:pad_r, 0:1], factor_b.shape)
    energy_b[...] = jnp.broadcast_to(columns[:pad_r, 1:2], energy_b.shape)

    for tile in range(tiles):
        state[tile, species:, :] = jnp.zeros((depth - species, tile_len), f32)
        for k in range(tile_rows):
            here = tile * tile_rows + k
            part = slice(k * width, (k + 1) * width)
            state[tile, :species, part] = spec_ref[:, here, :]
            state[tile, species : species + 1, part] = temp_ref[here : here + 1, :]

    def per_tile(tile, carry):
        count = tallies[0, tile]
        delta = step_time / jnp.full((1, lanes), count, jnp.int32).astype(f32)

        def step(turn, inner):
            for begin in range(0, tile_len, 256):
                now = state[tile, :, begin : begin + 256]
                top, low = halves(now)
                operand = jnp.concatenate([top, low, top], axis=0)
                progress = jnp.dot(gather_w[...], operand, preferred_element_type=f32)
                inverse = 1.0 / (1.0 + jnp.abs(now[species : species + 1]))
                wide = lambda ref: jnp.concatenate([ref[...]] * (256 // lanes), axis=1)
                rates = jnp.exp2(wide(factor_b) - wide(energy_b) * inverse)
                flux_hi, flux_lo = halves(rates * progress)
                first = jnp.dot(scatter_hi[...], flux_hi, preferred_element_type=f32)
                second = jnp.dot(scatter_lo[...], flux_lo, preferred_element_type=f32)
                change = first[:depth] + first[depth:] + second
                state[tile, :, begin : begin + 256] = now + jnp.concatenate([delta] * (256 // lanes), axis=1) * change
            return inner

        return lax.fori_loop(0, count, step, carry)

    lax.fori_loop(0, tiles, per_tile, 0)

    lane = lax.broadcasted_iota(jnp.int32, share_out.shape, 1)
    shares = jnp.zeros(share_out.shape, f32)
    for tile in range(tiles):
        for k in range(tile_rows):
            here = tile * tile_rows + k
            part = slice(k * width, (k + 1) * width)
            spec_out[:, here, :] = state[tile, :species, part]
            temp_out[here : here + 1, :] = state[tile, species : species + 1, part]
            rhs_out[here : here + 1, :] = (
                flow_ref[here : here + 1, :] + state[tile, species + 1 : species + 2, part]
            )
        heat = state[tile, species + 1 : species + 2, :]
        total = jnp.sum(heat * heat, axis=1, keepdims=True)
        shares = shares + jnp.where(lane == owners[0, tile], total, 0.0)
    share_out[...] = shares


def chemistry(spec, temp, flow, tallies, owners, consumed, molar, factor, energy, enthalpy):
    species, rows, width = spec.shape
    reactions = consumed.shape[0]
    tiles = tallies.shape[1]
    depth = round_up(species + 2, 64)
    pad_r = round_up(reactions, 16)
    smem = pl.BlockSpec(memory_space=pltpu.SMEM)
    vmem = pl.BlockSpec(memory_space=pltpu.VMEM)
    return pl.pallas_call(
        functools.partial(chemistry_kernel, tiles=tiles),
        out_shape=(
            jax.ShapeDtypeStruct(spec.shape, f32),
            jax.ShapeDtypeStruct(temp.shape, f32),
            jax.ShapeDtypeStruct(temp.shape, f32),
            jax.ShapeDtypeStruct((8, width), f32),
        ),
        in_specs=[smem, smem] + [vmem] * 8,
        out_specs=[vmem] * 4,
        scratch_shapes=[
            pltpu.VMEM((tiles, depth, rows * width // tiles), f32),
            pltpu.VMEM((pad_r, 3 * depth), bf16),
            pltpu.VMEM((2 * depth, pad_r), bf16),
            pltpu.VMEM((depth, pad_r), bf16),
            pltpu.VMEM((pad_r, lanes), f32),
            pltpu.VMEM((pad_r, lanes), f32),
            pltpu.VMEM((round_up(reactions, lanes), lanes), f32),
        ],
        name="chemistry",
    )(
        tallies,
        owners,
        spec,
        temp,
        flow,
        consumed,
        molar,
        factor[None],
        energy[None],
        enthalpy[None],
    )


def join_kernel(rhs_ref, share_ref, a_ref, b_ref, out_ref, *, reach):
    width = rhs_ref.shape[1]
    even = lax.axis_index("gy") % 2 == 0
    right = jnp.where(even, a_ref[...], b_ref[...])
    left = jnp.where(even, b_ref[...], a_ref[...])
    lane = lax.broadcasted_iota(jnp.int32, rhs_ref.shape, 1)
    side = jnp.where(lane < reach, right, left)
    out_ref[:, :width] = rhs_ref[...]
    out_ref[:, width:] = side
    out_ref[0:1, width:] = jnp.where(
        (lane[0:1] < reach) | (lane[0:1] >= width - reach),
        side[0:1],
        pltpu.roll(share_ref[0:1, :], reach, 1),
    )


def join_sides(rhs, shares, a, b, reach):
    rows, width = rhs.shape
    vmem = pl.BlockSpec(memory_space=pltpu.VMEM)
    return pl.pallas_call(
        functools.partial(join_kernel, reach=reach),
        out_shape=jax.ShapeDtypeStruct((rows, 2 * width), f32),
        in_specs=[vmem] * 4,
        out_specs=vmem,
        name="join_sides",
    )(rhs, shares, a, b)


def multigrid_kernel(*refs, reach, quick, count_x, count_y):
    if quick:
        mid_ref, a_ref, b_ref, share_ref, out_ref, burden_ref = refs
    else:
        mid_ref, a_ref, b_ref, out_ref = refs
    rows = mid_ref.shape[0]
    width = mid_ref.shape[1] // 2
    at_x = lax.axis_index("gx")
    at_y = lax.axis_index("gy")
    if quick:
        own = (
            mid_ref[0:1, width:]
            + a_ref[0:1, width:]
            + b_ref[0:1, width:]
            + pltpu.roll(share_ref[0:1, :], reach, 1)
        )
        lane = lax.broadcasted_iota(jnp.int32, own.shape, 1)
        own = jnp.where(lane == at_x + reach, own, 0.0)
        burden_ref[...] = jnp.sum(own, axis=1, keepdims=True) / (rows * width)

    even = at_x % 2 == 0
    above = jnp.where(even, b_ref[...], a_ref[...])
    below = jnp.where(even, a_ref[...], b_ref[...])
    whole = jnp.concatenate([above, mid_ref[...], below], axis=0)
    tall, wide = whole.shape
    down = lax.broadcasted_iota(jnp.int32, whole.shape, 0)
    across = lax.broadcasted_iota(jnp.int32, whole.shape, 1)
    row = at_x * rows + down - rows
    column = at_y * width + jnp.where(across >= width + width // 2, across - wide, across)
    inside = (row >= 0) & (row < count_x * rows) & (column >= 0) & (column < count_y * width)
    keep = jnp.where(inside, relax / 4.0, 0.0)
    whole = jnp.where(inside, whole, 0.0)

    def beside(field, step):
        return (
            pltpu.roll(field, step, 0)
            + pltpu.roll(field, tall - step, 0)
            + pltpu.roll(field, step, 1)
            + pltpu.roll(field, wide - step, 1)
        )

    def halve(field, step):
        odd = (down & step) != 0
        field = field + jnp.where(odd, pltpu.roll(field, step, 0), pltpu.roll(field, tall - step, 0))
        odd = (across & step) != 0
        field = field + jnp.where(odd, pltpu.roll(field, step, 1), pltpu.roll(field, wide - step, 1))
        return 0.25 * field

    def smooth(field, source, step):
        return keep * ((field + source) + beside(field, step))

    def vcycle(rhs, level):
        step = 2**level
        scale = 4.0**level
        source = scale * rhs
        field = keep * source
        if level == LEVELS - 1:
            for turn in range(COARSE - 1):
                field = smooth(field, source, step)
            return field
        for turn in range(SWEEPS - 1):
            field = smooth(field, source, step)
        resid = rhs - (4.0 * field - beside(field, step)) / scale
        field = field + vcycle(halve(resid, step), level + 1)
        for turn in range(SWEEPS):
            field = smooth(field, source, step)
        return field

    out_ref[...] = vcycle(whole, 0)[rows : 2 * rows, :width]


def multigrid(mid, a, b, shares, reach, count_x, count_y):
    rows = mid.shape[0]
    width = mid.shape[1] // 2
    quick = shares is not None
    vmem = pl.BlockSpec(memory_space=pltpu.VMEM)
    field = jax.ShapeDtypeStruct((rows, width), f32)
    return pl.pallas_call(
        functools.partial(
            multigrid_kernel, reach=reach, quick=quick, count_x=count_x, count_y=count_y
        ),
        out_shape=(field, jax.ShapeDtypeStruct((1, 1), f32)) if quick else field,
        in_specs=[vmem] * (4 if quick else 3),
        out_specs=(vmem, vmem) if quick else vmem,
        name="multigrid",
    )(*((mid, a, b, shares) if quick else (mid, a, b)))


def paired(axis, first):
    count = lax.axis_size(axis)
    pairs = []
    for low in range(first, count + first, 2):
        one, other = low % count, (low + 1) % count
        pairs += [(one, other), (other, one)]
    return pairs


def shards(
    chemical_concentration,
    thermal_scaled,
    tentative_flow_spread,
    substep_numbers,
    patch_holder_lookup,
    consumed_weighting,
    molar_coefficient,
    frequency_factor_log,
    arrhenius_energy,
    enthalpy_released,
):
    count_x, count_y = lax.axis_size("gx"), lax.axis_size("gy")
    rows, width = thermal_scaled.shape
    spec_new, temp_new, rhs, shares = chemistry(
        chemical_concentration,
        thermal_scaled,
        tentative_flow_spread,
        substep_numbers,
        patch_holder_lookup,
        consumed_weighting,
        molar_coefficient,
        frequency_factor_log,
        arrhenius_energy,
        enthalpy_released,
    )
    reach = 32
    quick = count_x == 4
    far = lax.ppermute(shares, "gx", [(i, i ^ 2) for i in range(4)]) if quick else None
    side_a = lax.ppermute(rhs, "gy", paired("gy", 0))
    side_b = lax.ppermute(rhs, "gy", paired("gy", 1))
    band = join_sides(rhs, shares, side_a, side_b, reach)
    band_a = lax.ppermute(band, "gx", paired("gx", 0))
    band_b = lax.ppermute(band, "gx", paired("gx", 1))
    if quick:
        field, burden = multigrid(band, band_a, band_b, far, reach, count_x, count_y)
    else:
        field = multigrid(band, band_a, band_b, None, reach, count_x, count_y)
        burden = lax.psum_scatter(
            shares[0, :count_x], "gx", scatter_dimension=0, tiled=True
        ).reshape(1, 1) / (rows * width)
    return spec_new, temp_new, field, burden


def solution(mesh):
    return jax.shard_map(
        shards,
        mesh=mesh,
        in_specs=(
            P(None, "gx", "gy"),
            P("gx", "gy"),
            P("gx", "gy"),
            P("gx", "gy"),
            P("gx", "gy"),
            P(),
            P(),
            P(),
            P(),
            P(),
        ),
        out_specs=(P(None, "gx", "gy"), P("gx", "gy"), P("gx", "gy"), P("gx", "gy")),
        check_vma=False,
    )
```

```python
import functools
import math

import jax
import jax.numpy as jnp
from jax import lax
from jax.experimental import pallas as pl
from jax.experimental.pallas import tpu as pltpu
from jax.sharding import PartitionSpec as P

LEVELS = 3
SWEEPS = 2
COARSE = 4

step_time = 0.4
relax = 0.8
lanes = 128
log2e = math.log2(math.e)
f32 = jnp.float32
bf16 = jnp.bfloat16
high = lax.Precision.HIGHEST


def round_up(value, multiple):
    return -(-value // multiple) * multiple


def halves(value):
    top = value.astype(bf16)
    return top, (value - top.astype(f32)).astype(bf16)


def chemistry_kernel(
    tallies_hbm,
    owners_hbm,
    spec_hbm,
    temp_hbm,
    flow_hbm,
    consumed_hbm,
    molar_hbm,
    factor_hbm,
    energy_hbm,
    enthalpy_hbm,
    rhs_out,
    share_out,
    *rest,
    groups,
):
    states = rest[:groups]
    blocks = rest[groups : 2 * groups]
    (
        tallies,
        owners,
        temp_ref,
        flow_ref,
        consumed_ref,
        molar_ref,
        factor_ref,
        energy_ref,
        enthalpy_ref,
        gather_w,
        scatter_one,
        scatter_two,
        energy_b,
        staging,
        late_hi,
        late_lo,
        arrival,
    ) = rest[2 * groups :]
    species = spec_hbm.shape[0]
    reactions = consumed_ref.shape[1]
    depth, group_len = states[0].shape
    pad_s, group_rows, width = blocks[0].shape
    tiles = tallies.shape[1]
    tile_len = groups * group_len // tiles
    pad_r, reach = gather_w.shape[0], late_hi.shape[1]
    used = scatter_two.shape[0]
    spread = staging.shape[1]
    split = scatter_one.shape[1] - pad_r

    small = [
        (consumed_hbm, consumed_ref),
        (factor_hbm, factor_ref),
        (energy_hbm, energy_ref),
        (molar_hbm, molar_ref),
        (enthalpy_hbm, enthalpy_ref),
        (tallies_hbm, tallies),
        (owners_hbm, owners),
        (temp_hbm, temp_ref),
        (flow_hbm, flow_ref),
    ]
    small = [
        pltpu.make_async_copy(source, target, arrival.at[k])
        for k, (source, target) in enumerate(small)
    ]
    large = [
        pltpu.make_async_copy(
            spec_hbm.at[:, group * group_rows : (group + 1) * group_rows, :],
            block.at[:species],
            arrival.at[len(small) + group],
        )
        for group, block in enumerate(blocks)
    ]
    for copy in small + large:
        copy.start()

    def flat(ref):
        return jnp.pad(ref[...].reshape(1, reactions), ((0, 0), (0, spread - reactions)))

    staging[...] = jnp.zeros_like(staging)
    late_hi[...] = jnp.zeros_like(late_hi)
    late_lo[...] = jnp.zeros_like(late_lo)
    for copy in small:
        copy.wait()
    staging[:species, :reactions] = consumed_ref[...]
    weights = staging[...] * jnp.exp(flat(factor_ref))
    row = lax.broadcasted_iota(jnp.int32, weights.shape, 0)
    weights = jnp.where(row == species, flat(energy_ref) * -log2e, weights)
    columns = jnp.transpose(weights)[:pad_r]
    energy_b[...] = jnp.broadcast_to(columns[:, species : species + 1], energy_b.shape)
    lane = lax.broadcasted_iota(jnp.int32, columns.shape, 1)
    top, low = halves(jnp.where(lane < species, columns, 0.0)[:, :depth])
    gather_w[...] = jnp.concatenate([top, top, low], axis=1)
    staging[:species, :reactions] = molar_ref[...]
    enthalpy = flat(enthalpy_ref)
    weights = jnp.where((row == species) | (row == species + 1), enthalpy, staging[...])[:used]
    top = weights.astype(bf16).astype(f32)
    low = (weights - top)[:, :pad_r]
    top = top[:, :pad_r]
    scatter_one[...] = jnp.concatenate(
        [
            jnp.concatenate([top, top[:, :split]], axis=1),
            jnp.concatenate([low, jnp.zeros((used, split), f32)], axis=1),
        ],
        axis=0,
    ).astype(bf16)
    scatter_two[...] = top[:, split:].astype(bf16)

    for group, (state, block) in enumerate(zip(states, blocks)):
        large[group].wait()
        lines = block.reshape(pad_s * group_rows, width)
        state[species:, :] = jnp.zeros((depth - species, group_len), f32)
        for k in range(group_rows):
            here = group * group_rows + k
            part = slice(k * width, (k + 1) * width)
            state[:species, part] = lines[pl.ds(k, species, stride=group_rows), :]
            state[species : species + 1, part] = temp_ref[here : here + 1, :]

    def front(state, begin):
        now = state[:, begin : begin + reach]
        top, low = halves(now)
        operand = jnp.concatenate([top, low, top], axis=0)
        progress = jnp.dot(gather_w[...], operand, preferred_element_type=f32)
        inverse = 1.0 / (1.0 + jnp.abs(now[species : species + 1]))
        energy = jnp.concatenate([energy_b[...]] * (reach // lanes), axis=1)
        return halves(jnp.exp2(energy * inverse) * progress)

    counts = [tallies[0, tile] for tile in range(tiles)]
    turns = functools.reduce(jnp.maximum, counts)

    def per_cell(group, begin, turn):
        first = group * group_len + begin
        piece = min(tile_len, reach)
        row = []
        for cell in range(first, first + reach, piece):
            count = jnp.full((1, piece), counts[cell // tile_len], jnp.int32)
            row.append(jnp.where(turn < count, step_time / count.astype(f32), 0.0))
        return jnp.concatenate(row, axis=1)

    def back(group, begin, flux, turn):
        flux_hi, flux_lo = flux
        operand = jnp.concatenate([flux_hi, flux_lo[:split]], axis=0)
        first = jnp.dot(scatter_one[...], operand, preferred_element_type=f32)
        second = jnp.dot(scatter_two[...], flux_lo[split:], preferred_element_type=f32)
        change = (first[:used] + first[used:]) + second
        states[group][:used, begin : begin + reach] += per_cell(group, begin, turn) * change

    work = [(group, begin) for group in range(groups) for begin in range(0, group_len, reach)]

    def step(turn, carry):
        pending = (*work[-1], (late_hi[...], late_lo[...]), turn - 1)
        for group, begin in work:
            flux = front(states[group], begin)
            back(*pending)
            pending = (group, begin, flux, turn)
        late_hi[...], late_lo[...] = pending[2]
        return carry

    lax.fori_loop(0, turns, step, 0)
    back(*work[-1], (late_hi[...], late_lo[...]), turns - 1)

    lane = lax.broadcasted_iota(jnp.int32, share_out.shape, 1)
    shares = jnp.zeros(share_out.shape, f32)
    for group, state in enumerate(states):
        heat = state[species + 1 : species + 2, :]
        for k in range(group_rows):
            here = group * group_rows + k
            part = slice(k * width, (k + 1) * width)
            rhs_out[here : here + 1, :] = flow_ref[here : here + 1, :] + heat[:, part]
        squares = heat * heat
        for cell in range(0, group_len, min(tile_len, group_len)):
            tile = (group * group_len + cell) // tile_len
            total = jnp.sum(squares[:, cell : cell + tile_len], axis=1, keepdims=True)
            shares = shares + jnp.where(lane == owners[0, tile], total, 0.0)
    share_out[...] = shares


def unpack_kernel(*refs, groups):
    states = refs[:groups]
    spec_hbm, temp_out = refs[groups : groups + 2]
    blocks = refs[groups + 2 : 2 * groups + 2]
    leave = refs[2 * groups + 2]
    species = spec_hbm.shape[0]
    pad_s, group_rows, width = blocks[0].shape
    copies = []
    for group, (state, block) in enumerate(zip(states, blocks)):
        lines = block.reshape(pad_s * group_rows, width)
        for k in range(group_rows):
            here = group * group_rows + k
            part = slice(k * width, (k + 1) * width)
            lines[pl.ds(k, pad_s, stride=group_rows), :] = state[:pad_s, part]
            temp_out[here : here + 1, :] = state[species : species + 1, part]
        copy = pltpu.make_async_copy(
            block.at[:species],
            spec_hbm.at[:, group * group_rows : (group + 1) * group_rows, :],
            leave.at[group],
        )
        copy.start()
        copies.append(copy)
    for copy in copies:
        copy.wait()


def chemistry(spec, temp, flow, tallies, owners, consumed, molar, factor, energy, enthalpy):
    species, rows, width = spec.shape
    reactions = consumed.shape[0]
    group_rows = 8
    groups = rows // group_rows
    group_len = group_rows * width
    depth = round_up(species + 2, 64)
    used = round_up(species + 2, 8)
    pad_r = round_up(reactions, 16)
    split = -pad_r % 256
    reach = 512
    hbm = pl.BlockSpec(memory_space=pltpu.HBM)
    vmem = pl.BlockSpec(memory_space=pltpu.VMEM)
    block = pltpu.VMEM((round_up(species, 8), group_rows, width), f32)
    rhs, shares, *states = pl.pallas_call(
        functools.partial(chemistry_kernel, groups=groups),
        out_shape=[
            jax.ShapeDtypeStruct(temp.shape, f32),
            jax.ShapeDtypeStruct((8, width), f32),
        ]
        + [jax.ShapeDtypeStruct((depth, group_len), f32)] * groups,
        in_specs=[hbm] * 10,
        out_specs=[vmem] * (2 + groups),
        scratch_shapes=[block] * groups
        + [
            pltpu.SMEM(tallies.shape, jnp.int32),
            pltpu.SMEM(owners.shape, jnp.int32),
            pltpu.VMEM(temp.shape, f32),
            pltpu.VMEM(flow.shape, f32),
            pltpu.VMEM((species, reactions), f32),
            pltpu.VMEM((species, reactions), f32),
            pltpu.VMEM((reactions,), f32),
            pltpu.VMEM((reactions,), f32),
            pltpu.VMEM((reactions,), f32),
            pltpu.VMEM((pad_r, 3 * depth), bf16),
            pltpu.VMEM((2 * used, pad_r + split), bf16),
            pltpu.VMEM((used, pad_r - split), bf16),
            pltpu.VMEM((pad_r, lanes), f32),
            pltpu.VMEM((lanes, round_up(reactions, lanes)), f32),
            pltpu.VMEM((pad_r, reach), bf16),
            pltpu.VMEM((pad_r, reach), bf16),
            pltpu.SemaphoreType.DMA((9 + groups,)),
        ],
        compiler_params=pltpu.CompilerParams(vmem_limit_bytes=24 << 20),
        name="chemistry",
    )(
        *(
            pltpu.with_memory_space_constraint(array, pltpu.HBM)
            for array in (
                tallies,
                owners,
                spec,
                temp,
                flow,
                consumed.T,
                molar.T,
                factor,
                energy,
                enthalpy,
            )
        )
    )
    spec_new, temp_new = pl.pallas_call(
        functools.partial(unpack_kernel, groups=groups),
        out_shape=[
            jax.ShapeDtypeStruct(spec.shape, f32),
            jax.ShapeDtypeStruct(temp.shape, f32),
        ],
        in_specs=[vmem] * groups,
        out_specs=[hbm, vmem],
        scratch_shapes=[block] * groups + [pltpu.SemaphoreType.DMA((groups,))],
        compiler_params=pltpu.CompilerParams(vmem_limit_bytes=4 << 20),
        cost_estimate=pl.CostEstimate(
            flops=spec.size, bytes_accessed=8 * spec.size, transcendentals=0
        ),
        name="unpack",
    )(*states)
    return spec_new, temp_new, rhs, shares


def join_kernel(rhs_ref, share_ref, a_ref, b_ref, out_ref, *, reach):
    width = rhs_ref.shape[1]
    even = lax.axis_index("gy") % 2 == 0
    right = jnp.where(even, a_ref[...], b_ref[...])
    left = jnp.where(even, b_ref[...], a_ref[...])
    lane = lax.broadcasted_iota(jnp.int32, rhs_ref.shape, 1)
    side = jnp.where(lane < reach, right, left)
    out_ref[:, :width] = rhs_ref[...]
    out_ref[:, width:] = side
    out_ref[0:1, width:] = jnp.where(
        (lane[0:1] < reach) | (lane[0:1] >= width - reach),
        side[0:1],
        pltpu.roll(share_ref[0:1, :], reach, 1),
    )


def join_sides(rhs, shares, a, b, reach):
    rows, width = rhs.shape
    vmem = pl.BlockSpec(memory_space=pltpu.VMEM)
    return pl.pallas_call(
        functools.partial(join_kernel, reach=reach),
        out_shape=jax.ShapeDtypeStruct((rows, 2 * width), f32),
        in_specs=[vmem] * 4,
        out_specs=vmem,
        compiler_params=pltpu.CompilerParams(vmem_limit_bytes=4 << 20),
        name="join_sides",
    )(rhs, shares, a, b)


def multigrid_kernel(*refs, reach, quick, count_x, count_y):
    if quick:
        mid_ref, a_ref, b_ref, share_ref, out_ref, burden_ref = refs
    else:
        mid_ref, a_ref, b_ref, out_ref = refs
    rows = mid_ref.shape[0]
    width = mid_ref.shape[1] // 2
    at_x = lax.axis_index("gx")
    at_y = lax.axis_index("gy")
    if quick:
        own = (
            mid_ref[0:1, width:]
            + a_ref[0:1, width:]
            + b_ref[0:1, width:]
            + pltpu.roll(share_ref[0:1, :], reach, 1)
        )
        lane = lax.broadcasted_iota(jnp.int32, own.shape, 1)
        own = jnp.where(lane == at_x + reach, own, 0.0)
        burden_ref[...] = jnp.sum(own, axis=1, keepdims=True) / (rows * width)

    even = at_x % 2 == 0
    above = jnp.where(even, b_ref[...], a_ref[...])
    below = jnp.where(even, a_ref[...], b_ref[...])
    whole = jnp.concatenate([above, mid_ref[...], below], axis=0)
    tall, wide = whole.shape
    down = lax.broadcasted_iota(jnp.int32, whole.shape, 0)
    across = lax.broadcasted_iota(jnp.int32, whole.shape, 1)
    row = at_x * rows + down - rows
    column = at_y * width + jnp.where(across >= width + width // 2, across - wide, across)
    inside = (row >= 0) & (row < count_x * rows) & (column >= 0) & (column < count_y * width)
    keep = jnp.where(inside, relax / 4.0, 0.0)
    whole = jnp.where(inside, whole, 0.0)

    def beside(field, step):
        return (
            pltpu.roll(field, step, 0)
            + pltpu.roll(field, tall - step, 0)
            + pltpu.roll(field, step, 1)
            + pltpu.roll(field, wide - step, 1)
        )

    def halve(field, step):
        odd = (down & step) != 0
        field = field + jnp.where(odd, pltpu.roll(field, step, 0), pltpu.roll(field, tall - step, 0))
        odd = (across & step) != 0
        field = field + jnp.where(odd, pltpu.roll(field, step, 1), pltpu.roll(field, wide - step, 1))
        return 0.25 * field

    def smooth(field, source, step):
        return keep * ((field + source) + beside(field, step))

    def vcycle(rhs, level):
        step = 2**level
        scale = 4.0**level
        source = scale * rhs
        field = keep * source
        if level == LEVELS - 1:
            for turn in range(COARSE - 1):
                field = smooth(field, source, step)
            return field
        for turn in range(SWEEPS - 1):
            field = smooth(field, source, step)
        resid = rhs - (4.0 * field - beside(field, step)) / scale
        field = field + vcycle(halve(resid, step), level + 1)
        for turn in range(SWEEPS):
            field = smooth(field, source, step)
        return field

    out_ref[...] = vcycle(whole, 0)[rows : 2 * rows, :width]


def multigrid(mid, a, b, shares, reach, count_x, count_y):
    rows = mid.shape[0]
    width = mid.shape[1] // 2
    quick = shares is not None
    vmem = pl.BlockSpec(memory_space=pltpu.VMEM)
    field = jax.ShapeDtypeStruct((rows, width), f32)
    return pl.pallas_call(
        functools.partial(
            multigrid_kernel, reach=reach, quick=quick, count_x=count_x, count_y=count_y
        ),
        out_shape=(field, jax.ShapeDtypeStruct((1, 1), f32)) if quick else field,
        in_specs=[vmem] * (4 if quick else 3),
        out_specs=(vmem, vmem) if quick else vmem,
        compiler_params=pltpu.CompilerParams(vmem_limit_bytes=8 << 20),
        name="multigrid",
    )(*((mid, a, b, shares) if quick else (mid, a, b)))


def paired(axis, first):
    count = lax.axis_size(axis)
    pairs = []
    for low in range(first, count + first, 2):
        one, other = low % count, (low + 1) % count
        pairs += [(one, other), (other, one)]
    return pairs


def shards(
    chemical_concentration,
    thermal_scaled,
    tentative_flow_spread,
    substep_numbers,
    patch_holder_lookup,
    consumed_weighting,
    molar_coefficient,
    frequency_factor_log,
    arrhenius_energy,
    enthalpy_released,
):
    count_x, count_y = lax.axis_size("gx"), lax.axis_size("gy")
    rows, width = thermal_scaled.shape
    spec_new, temp_new, rhs, shares = chemistry(
        chemical_concentration,
        thermal_scaled,
        tentative_flow_spread,
        substep_numbers,
        patch_holder_lookup,
        consumed_weighting,
        molar_coefficient,
        frequency_factor_log,
        arrhenius_energy,
        enthalpy_released,
    )
    reach = 32
    quick = count_x == 4
    far = lax.ppermute(shares, "gx", [(i, i ^ 2) for i in range(4)]) if quick else None
    side_a = lax.ppermute(rhs, "gy", paired("gy", 0))
    side_b = lax.ppermute(rhs, "gy", paired("gy", 1))
    band = join_sides(rhs, shares, side_a, side_b, reach)
    band_a = lax.ppermute(band, "gx", paired("gx", 0))
    band_b = lax.ppermute(band, "gx", paired("gx", 1))
    if quick:
        field, burden = multigrid(band, band_a, band_b, far, reach, count_x, count_y)
    else:
        field = multigrid(band, band_a, band_b, None, reach, count_x, count_y)
        burden = lax.psum_scatter(
            shares[0, :count_x], "gx", scatter_dimension=0, tiled=True
        ).reshape(1, 1) / (rows * width)
    return spec_new, temp_new, field, burden


def solution(mesh):
    return jax.shard_map(
        shards,
        mesh=mesh,
        in_specs=(
            P(None, "gx", "gy"),
            P("gx", "gy"),
            P("gx", "gy"),
            P("gx", "gy"),
            P("gx", "gy"),
            P(),
            P(),
            P(),
            P(),
            P(),
        ),
        out_specs=(P(None, "gx", "gy"), P("gx", "gy"), P("gx", "gy"), P("gx", "gy")),
        check_vma=False,
    )
```

```python
import functools
import math

import jax
import jax.numpy as jnp
from jax import lax
from jax.experimental import pallas as pl
from jax.experimental.pallas import tpu as pltpu
from jax.sharding import PartitionSpec as P


LEVELS = 3
SWEEPS = 2
COARSE = 4

step_time = 0.4
relax = 0.8
lanes = 128
log2e = math.log2(math.e)
f32 = jnp.float32
bf16 = jnp.bfloat16


def round_up(value, multiple):
    return -(-value // multiple) * multiple


def halves(value):
    top = value.astype(bf16)
    return top, (value - top.astype(f32)).astype(bf16)


def chemistry_kernel(
    tallies_hbm,
    owners_hbm,
    spec_hbm,
    temp_hbm,
    flow_hbm,
    consumed_hbm,
    molar_hbm,
    factor_hbm,
    energy_hbm,
    enthalpy_hbm,
    rhs_out,
    share_out,
    *rest,
    groups,
):
    states = rest[:groups]
    blocks = rest[groups : 2 * groups]
    (
        tallies,
        owners,
        temp_ref,
        flow_ref,
        consumed_ref,
        molar_ref,
        factor_ref,
        energy_ref,
        enthalpy_ref,
        gather_w,
        scatter_one,
        scatter_two,
        energy_b,
        staging,
        late_hi,
        late_lo,
        ahead,
        arrival,
    ) = rest[2 * groups :]
    species = spec_hbm.shape[0]
    reactions = consumed_ref.shape[1]
    depth, group_len = states[0].shape
    pad_s, group_rows, width = blocks[0].shape
    tiles = tallies.shape[1]
    tile_len = groups * group_len // tiles
    pad_r, reach = gather_w.shape[0], late_hi.shape[1]
    used = scatter_two.shape[0]
    spread = staging.shape[1]
    deep = scatter_one.shape[1]

    small = [
        (consumed_hbm, consumed_ref),
        (factor_hbm, factor_ref),
        (energy_hbm, energy_ref),
        (molar_hbm, molar_ref),
        (enthalpy_hbm, enthalpy_ref),
        (tallies_hbm, tallies),
        (owners_hbm, owners),
        (temp_hbm, temp_ref),
        (flow_hbm, flow_ref),
    ]
    small = [
        pltpu.make_async_copy(source, target, arrival.at[k])
        for k, (source, target) in enumerate(small)
    ]
    large = [
        pltpu.make_async_copy(
            spec_hbm.at[:, group * group_rows : (group + 1) * group_rows, :],
            block.at[:species],
            arrival.at[len(small) + group],
        )
        for group, block in enumerate(blocks)
    ]
    for copy in small + large:
        copy.start()

    def flat(ref):
        return jnp.pad(ref[...].reshape(1, reactions), ((0, 0), (0, spread - reactions)))

    staging[...] = jnp.zeros_like(staging)
    late_hi[...] = jnp.zeros_like(late_hi)
    late_lo[...] = jnp.zeros_like(late_lo)
    for copy in small:
        copy.wait()
    staging[:species, :reactions] = consumed_ref[...]
    weights = staging[...] * jnp.exp(flat(factor_ref))
    row = lax.broadcasted_iota(jnp.int32, weights.shape, 0)
    weights = jnp.where(row == species, flat(energy_ref) * -log2e, weights)
    columns = jnp.transpose(weights)[:pad_r]
    energy_b[...] = jnp.broadcast_to(columns[:, species : species + 1], energy_b.shape)
    lane = lax.broadcasted_iota(jnp.int32, columns.shape, 1)
    top, low = halves(jnp.where(lane < species, columns, 0.0)[:, :depth])
    gather_w[...] = jnp.concatenate([top, top, low], axis=1)
    staging[:species, :reactions] = molar_ref[...]
    enthalpy = flat(enthalpy_ref)
    weights = jnp.where((row == species) | (row == species + 1), enthalpy, staging[...])[:used]
    top = weights.astype(bf16).astype(f32)
    low = (weights - top)[:, :pad_r]
    top = top[:, :pad_r]
    scatter_one[...] = jnp.concatenate([top[:, :deep], low[:, :deep]], axis=0).astype(bf16)
    scatter_two[...] = jnp.concatenate([top[:, deep:], top, low[:, deep:]], axis=1).astype(bf16)

    for group, (state, block) in enumerate(zip(states, blocks)):
        large[group].wait()
        lines = block.reshape(pad_s * group_rows, width)
        state[species:, :] = jnp.zeros((depth - species, group_len), f32)
        for k in range(group_rows):
            here = group * group_rows + k
            part = slice(k * width, (k + 1) * width)
            state[:species, part] = lines[pl.ds(k, species, stride=group_rows), :]
            state[species : species + 1, part] = temp_ref[here : here + 1, :]

    def spend(group, begin):
        top, low = halves(states[group][:, begin : begin + reach])
        operand = jnp.concatenate([top, low, top], axis=0)
        return jnp.dot(gather_w[...], operand, preferred_element_type=f32)

    def react(group, begin, progress):
        heat = states[group][species : species + 1, begin : begin + reach]
        inverse = 1.0 / (1.0 + jnp.abs(heat))
        energy = jnp.concatenate([energy_b[...]] * (reach // lanes), axis=1)
        return halves(jnp.exp2(energy * inverse) * progress)

    counts = [tallies[0, tile] for tile in range(tiles)]
    turns = functools.reduce(jnp.maximum, counts)

    def per_cell(group, begin, turn):
        first = group * group_len + begin
        piece = min(tile_len, reach)
        row = []
        for cell in range(first, first + reach, piece):
            count = jnp.full((1, piece), counts[cell // tile_len], jnp.int32)
            row.append(jnp.where(turn < count, step_time / count.astype(f32), 0.0))
        return jnp.concatenate(row, axis=1)

    def back(group, begin, flux, turn):
        flux_hi, flux_lo = flux
        operand = jnp.concatenate([flux_hi[deep:], flux_lo, flux_hi[deep:]], axis=0)
        first = jnp.dot(scatter_one[...], flux_hi[:deep], preferred_element_type=f32)
        second = jnp.dot(scatter_two[...], operand, preferred_element_type=f32)
        change = (first[:used] + first[used:]) + second
        states[group][:used, begin : begin + reach] += per_cell(group, begin, turn) * change

    work = [(group, begin) for group in range(groups) for begin in range(0, group_len, reach)]

    def step(turn, carry):
        pending = (*work[-1], (late_hi[...], late_lo[...]), turn - 1)
        progress = ahead[...]
        for here, after in zip(work, work[1:] + work[:1]):
            coming = spend(*after)
            back(*pending)
            pending = (*here, react(*here, progress), turn)
            progress = coming
        ahead[...] = progress
        late_hi[...], late_lo[...] = pending[2]
        return carry

    ahead[...] = spend(*work[0])
    lax.fori_loop(0, turns, step, 0)
    back(*work[-1], (late_hi[...], late_lo[...]), turns - 1)

    lane = lax.broadcasted_iota(jnp.int32, share_out.shape, 1)
    shares = jnp.zeros(share_out.shape, f32)
    for group, state in enumerate(states):
        heat = state[species + 1 : species + 2, :]
        for k in range(group_rows):
            here = group * group_rows + k
            part = slice(k * width, (k + 1) * width)
            rhs_out[here : here + 1, :] = flow_ref[here : here + 1, :] + heat[:, part]
        squares = heat * heat
        for cell in range(0, group_len, min(tile_len, group_len)):
            tile = (group * group_len + cell) // tile_len
            total = jnp.sum(squares[:, cell : cell + tile_len], axis=1, keepdims=True)
            shares = shares + jnp.where(lane == owners[0, tile], total, 0.0)
    share_out[...] = shares


def unpack_kernel(*refs, groups):
    states = refs[:groups]
    spec_hbm, temp_out = refs[groups : groups + 2]
    blocks = refs[groups + 2 : 2 * groups + 2]
    leave = refs[2 * groups + 2]
    species = spec_hbm.shape[0]
    pad_s, group_rows, width = blocks[0].shape
    copies = []
    for group, (state, block) in enumerate(zip(states, blocks)):
        lines = block.reshape(pad_s * group_rows, width)
        for k in range(group_rows):
            here = group * group_rows + k
            part = slice(k * width, (k + 1) * width)
            lines[pl.ds(k, pad_s, stride=group_rows), :] = state[:pad_s, part]
            temp_out[here : here + 1, :] = state[species : species + 1, part]
        copy = pltpu.make_async_copy(
            block.at[:species],
            spec_hbm.at[:, group * group_rows : (group + 1) * group_rows, :],
            leave.at[group],
        )
        copy.start()
        copies.append(copy)
    for copy in copies:
        copy.wait()


def chemistry(spec, temp, flow, tallies, owners, consumed, molar, factor, energy, enthalpy):
    species, rows, width = spec.shape
    reactions = consumed.shape[0]
    group_rows = 8
    groups = rows // group_rows
    group_len = group_rows * width
    depth = round_up(species + 2, 64)
    used = round_up(species + 2, 8)
    pad_r = round_up(reactions, 16)
    deep = pad_r // 256 * 256
    reach = 256
    hbm = pl.BlockSpec(memory_space=pltpu.HBM)
    vmem = pl.BlockSpec(memory_space=pltpu.VMEM)
    block = pltpu.VMEM((round_up(species, 8), group_rows, width), f32)
    rhs, shares, *states = pl.pallas_call(
        functools.partial(chemistry_kernel, groups=groups),
        out_shape=[
            jax.ShapeDtypeStruct(temp.shape, f32),
            jax.ShapeDtypeStruct((8, width), f32),
        ]
        + [jax.ShapeDtypeStruct((depth, group_len), f32)] * groups,
        in_specs=[hbm] * 10,
        out_specs=[vmem] * (2 + groups),
        scratch_shapes=[block] * groups
        + [
            pltpu.SMEM(tallies.shape, jnp.int32),
            pltpu.SMEM(owners.shape, jnp.int32),
            pltpu.VMEM(temp.shape, f32),
            pltpu.VMEM(flow.shape, f32),
            pltpu.VMEM((species, reactions), f32),
            pltpu.VMEM((species, reactions), f32),
            pltpu.VMEM((reactions,), f32),
            pltpu.VMEM((reactions,), f32),
            pltpu.VMEM((reactions,), f32),
            pltpu.VMEM((pad_r, 3 * depth), bf16),
            pltpu.VMEM((2 * used, deep), bf16),
            pltpu.VMEM((used, 3 * pad_r - 2 * deep), bf16),
            pltpu.VMEM((pad_r, lanes), f32),
            pltpu.VMEM((lanes, round_up(reactions, lanes)), f32),
            pltpu.VMEM((pad_r, reach), bf16),
            pltpu.VMEM((pad_r, reach), bf16),
            pltpu.VMEM((pad_r, reach), f32),
            pltpu.SemaphoreType.DMA((9 + groups,)),
        ],
        compiler_params=pltpu.CompilerParams(vmem_limit_bytes=24 << 20),
        name="chemistry",
    )(
        *(
            pltpu.with_memory_space_constraint(array, pltpu.HBM)
            for array in (
                tallies,
                owners,
                spec,
                temp,
                flow,
                consumed.T,
                molar.T,
                factor,
                energy,
                enthalpy,
            )
        )
    )
    spec_new, temp_new = pl.pallas_call(
        functools.partial(unpack_kernel, groups=groups),
        out_shape=[
            jax.ShapeDtypeStruct(spec.shape, f32),
            jax.ShapeDtypeStruct(temp.shape, f32),
        ],
        in_specs=[vmem] * groups,
        out_specs=[hbm, vmem],
        scratch_shapes=[block] * groups + [pltpu.SemaphoreType.DMA((groups,))],
        compiler_params=pltpu.CompilerParams(vmem_limit_bytes=4 << 20),
        cost_estimate=pl.CostEstimate(
            flops=spec.size, bytes_accessed=8 * spec.size, transcendentals=0
        ),
        name="unpack",
    )(*states)
    return spec_new, temp_new, rhs, shares


def join_kernel(rhs_ref, share_ref, a_ref, b_ref, out_ref, *, reach):
    width = rhs_ref.shape[1]
    even = lax.axis_index("gy") % 2 == 0
    right = jnp.where(even, a_ref[...], b_ref[...])
    left = jnp.where(even, b_ref[...], a_ref[...])
    lane = lax.broadcasted_iota(jnp.int32, rhs_ref.shape, 1)
    side = jnp.where(lane < reach, right, left)
    out_ref[:, :width] = rhs_ref[...]
    out_ref[:, width:] = side
    out_ref[0:1, width:] = jnp.where(
        (lane[0:1] < reach) | (lane[0:1] >= width - reach),
        side[0:1],
        pltpu.roll(share_ref[0:1, :], reach, 1),
    )


def join_sides(rhs, shares, a, b, reach):
    rows, width = rhs.shape
    vmem = pl.BlockSpec(memory_space=pltpu.VMEM)
    return pl.pallas_call(
        functools.partial(join_kernel, reach=reach),
        out_shape=jax.ShapeDtypeStruct((rows, 2 * width), f32),
        in_specs=[vmem] * 4,
        out_specs=vmem,
        compiler_params=pltpu.CompilerParams(vmem_limit_bytes=4 << 20),
        name="join_sides",
    )(rhs, shares, a, b)


def multigrid_kernel(*refs, reach, quick, count_x, count_y):
    if quick:
        mid_ref, a_ref, b_ref, share_ref, out_ref, burden_ref = refs
    else:
        mid_ref, a_ref, b_ref, out_ref = refs
    rows = mid_ref.shape[0]
    width = mid_ref.shape[1] // 2
    at_x = lax.axis_index("gx")
    at_y = lax.axis_index("gy")
    if quick:
        own = (
            mid_ref[0:1, width:]
            + a_ref[0:1, width:]
            + b_ref[0:1, width:]
            + pltpu.roll(share_ref[0:1, :], reach, 1)
        )
        lane = lax.broadcasted_iota(jnp.int32, own.shape, 1)
        own = jnp.where(lane == at_x + reach, own, 0.0)
        burden_ref[...] = jnp.sum(own, axis=1, keepdims=True) / (rows * width)

    even = at_x % 2 == 0
    above = jnp.where(even, b_ref[...], a_ref[...])
    below = jnp.where(even, a_ref[...], b_ref[...])
    whole = jnp.concatenate([above, mid_ref[...], below], axis=0)
    tall, wide = whole.shape
    down = lax.broadcasted_iota(jnp.int32, whole.shape, 0)
    across = lax.broadcasted_iota(jnp.int32, whole.shape, 1)
    row = at_x * rows + down - rows
    column = at_y * width + jnp.where(across >= width + width // 2, across - wide, across)
    inside = (row >= 0) & (row < count_x * rows) & (column >= 0) & (column < count_y * width)
    keep = jnp.where(inside, relax / 4.0, 0.0)
    whole = jnp.where(inside, whole, 0.0)

    def beside(field, step):
        return (
            pltpu.roll(field, step, 0)
            + pltpu.roll(field, tall - step, 0)
            + pltpu.roll(field, step, 1)
            + pltpu.roll(field, wide - step, 1)
        )

    def halve(field, step):
        odd = (down & step) != 0
        field = field + jnp.where(odd, pltpu.roll(field, step, 0), pltpu.roll(field, tall - step, 0))
        odd = (across & step) != 0
        field = field + jnp.where(odd, pltpu.roll(field, step, 1), pltpu.roll(field, wide - step, 1))
        return 0.25 * field

    def smooth(field, source, step):
        return keep * ((field + source) + beside(field, step))

    def vcycle(rhs, level):
        step = 2**level
        scale = 4.0**level
        source = scale * rhs
        field = keep * source
        if level == LEVELS - 1:
            for _ in range(COARSE - 1):
                field = smooth(field, source, step)
            return field
        for _ in range(SWEEPS - 1):
            field = smooth(field, source, step)
        resid = rhs - (4.0 * field - beside(field, step)) / scale
        field = field + vcycle(halve(resid, step), level + 1)
        for _ in range(SWEEPS):
            field = smooth(field, source, step)
        return field

    out_ref[...] = vcycle(whole, 0)[rows : 2 * rows, :width]


def multigrid(mid, a, b, shares, reach, count_x, count_y):
    rows = mid.shape[0]
    width = mid.shape[1] // 2
    quick = shares is not None
    vmem = pl.BlockSpec(memory_space=pltpu.VMEM)
    field = jax.ShapeDtypeStruct((rows, width), f32)
    return pl.pallas_call(
        functools.partial(
            multigrid_kernel, reach=reach, quick=quick, count_x=count_x, count_y=count_y
        ),
        out_shape=(field, jax.ShapeDtypeStruct((1, 1), f32)) if quick else field,
        in_specs=[vmem] * (4 if quick else 3),
        out_specs=(vmem, vmem) if quick else vmem,
        compiler_params=pltpu.CompilerParams(vmem_limit_bytes=8 << 20),
        name="multigrid",
    )(*((mid, a, b, shares) if quick else (mid, a, b)))


def paired(axis, first, wrap=False):
    count = lax.axis_size(axis)
    pairs = []
    for low in range(first, count + first, 2):
        one, other = low % count, (low + 1) % count
        if one < other or wrap:
            pairs += [(one, other), (other, one)]
    return pairs


def shards(
    chemical_concentration,
    thermal_scaled,
    tentative_flow_spread,
    substep_numbers,
    patch_holder_lookup,
    consumed_weighting,
    molar_coefficient,
    frequency_factor_log,
    arrhenius_energy,
    enthalpy_released,
):
    count_x, count_y = lax.axis_size("gx"), lax.axis_size("gy")
    rows, width = thermal_scaled.shape
    spec_new, temp_new, rhs, shares = chemistry(
        chemical_concentration,
        thermal_scaled,
        tentative_flow_spread,
        substep_numbers,
        patch_holder_lookup,
        consumed_weighting,
        molar_coefficient,
        frequency_factor_log,
        arrhenius_energy,
        enthalpy_released,
    )
    reach = 32
    quick = count_x == 4
    far = None
    if quick:
        far = lax.ppermute(shares, "gx", [(i, i ^ 2) for i in range(4)])
    side_a = lax.ppermute(rhs, "gy", paired("gy", 0))
    side_b = lax.ppermute(rhs, "gy", paired("gy", 1))
    band = join_sides(rhs, shares, side_a, side_b, reach)
    band_a = lax.ppermute(band, "gx", paired("gx", 0))
    band_b = lax.ppermute(band, "gx", paired("gx", 1, wrap=quick))
    if quick:
        field, burden = multigrid(band, band_a, band_b, far, reach, count_x, count_y)
    else:
        field = multigrid(band, band_a, band_b, None, reach, count_x, count_y)
        burden = lax.psum_scatter(
            shares[0, :count_x], "gx", scatter_dimension=0, tiled=True
        ).reshape(1, 1) / (rows * width)
    return spec_new, temp_new, field, burden


def solution(mesh):
    return jax.shard_map(
        shards,
        mesh=mesh,
        in_specs=(
            P(None, "gx", "gy"),
            P("gx", "gy"),
            P("gx", "gy"),
            P("gx", "gy"),
            P("gx", "gy"),
            P(),
            P(),
            P(),
            P(),
            P(),
        ),
        out_specs=(P(None, "gx", "gy"), P("gx", "gy"), P("gx", "gy"), P("gx", "gy")),
        check_vma=False,
    )
```

```python
import functools
import math

import jax
import jax.numpy as jnp
from jax import lax
from jax.experimental import pallas as pl
from jax.experimental.pallas import tpu as pltpu
from jax.sharding import PartitionSpec as P


LEVELS = 3
SWEEPS = 2
COARSE = 4

step_time = 0.4
relax = 0.8
lanes = 128
log2e = math.log2(math.e)
f32 = jnp.float32
bf16 = jnp.bfloat16


def round_up(value, multiple):
    return -(-value // multiple) * multiple


def halves(value):
    top = value.astype(bf16)
    return top, (value - top.astype(f32)).astype(bf16)


def chemistry_kernel(
    tallies_hbm,
    owners_hbm,
    spec_hbm,
    temp_hbm,
    flow_hbm,
    consumed_hbm,
    molar_hbm,
    factor_hbm,
    energy_hbm,
    enthalpy_hbm,
    rhs_out,
    share_out,
    *rest,
    groups,
):
    states = rest[:groups]
    blocks = rest[groups : 2 * groups]
    (
        tallies,
        owners,
        temp_ref,
        flow_ref,
        consumed_ref,
        molar_ref,
        factor_ref,
        energy_ref,
        enthalpy_ref,
        gather_w,
        scatter_one,
        scatter_two,
        energy_b,
        staging,
        late_hi,
        late_lo,
        ahead,
        arrival,
    ) = rest[2 * groups :]
    species = spec_hbm.shape[0]
    reactions = consumed_ref.shape[1]
    depth, group_len = states[0].shape
    pad_s, group_rows, width = blocks[0].shape
    tiles = tallies.shape[1]
    tile_len = groups * group_len // tiles
    pad_r, reach = gather_w.shape[0], late_hi.shape[1]
    used = scatter_two.shape[0]
    spread = staging.shape[1]
    deep = scatter_one.shape[1]

    small = [
        (consumed_hbm, consumed_ref),
        (factor_hbm, factor_ref),
        (energy_hbm, energy_ref),
        (molar_hbm, molar_ref),
        (enthalpy_hbm, enthalpy_ref),
        (tallies_hbm, tallies),
        (owners_hbm, owners),
        (temp_hbm, temp_ref),
        (flow_hbm, flow_ref),
    ]
    small = [
        pltpu.make_async_copy(source, target, arrival.at[k])
        for k, (source, target) in enumerate(small)
    ]
    large = [
        pltpu.make_async_copy(
            spec_hbm.at[:, group * group_rows : (group + 1) * group_rows, :],
            block.at[:species],
            arrival.at[len(small) + group],
        )
        for group, block in enumerate(blocks)
    ]
    for copy in small + large:
        copy.start()

    def flat(ref):
        return jnp.pad(ref[...].reshape(1, reactions), ((0, 0), (0, spread - reactions)))

    staging[...] = jnp.zeros_like(staging)
    late_hi[...] = jnp.zeros_like(late_hi)
    late_lo[...] = jnp.zeros_like(late_lo)
    for copy in small:
        copy.wait()
    staging[:species, :reactions] = consumed_ref[...]
    weights = staging[...] * jnp.exp(flat(factor_ref))
    row = lax.broadcasted_iota(jnp.int32, weights.shape, 0)
    weights = jnp.where(row == species, flat(energy_ref) * -log2e, weights)
    columns = jnp.transpose(weights)[:pad_r]
    energy_b[...] = jnp.broadcast_to(columns[:, species : species + 1], energy_b.shape)
    lane = lax.broadcasted_iota(jnp.int32, columns.shape, 1)
    top, low = halves(jnp.where(lane < species, columns, 0.0)[:, :depth])
    gather_w[...] = jnp.concatenate([top, top, low], axis=1)
    staging[:species, :reactions] = molar_ref[...]
    enthalpy = flat(enthalpy_ref)
    weights = jnp.where((row == species) | (row == species + 1), enthalpy, staging[...])[:used]
    top = weights.astype(bf16).astype(f32)
    low = (weights - top)[:, :pad_r]
    top = top[:, :pad_r]
    scatter_one[...] = jnp.concatenate([top[:, :deep], low[:, :deep]], axis=0).astype(bf16)
    scatter_two[...] = jnp.concatenate([top[:, deep:], top, low[:, deep:]], axis=1).astype(bf16)

    for group, (state, block) in enumerate(zip(states, blocks)):
        large[group].wait()
        lines = block.reshape(pad_s * group_rows, width)
        state[species:, :] = jnp.zeros((depth - species, group_len), f32)
        for k in range(group_rows):
            here = group * group_rows + k
            part = slice(k * width, (k + 1) * width)
            state[:species, part] = lines[pl.ds(k, species, stride=group_rows), :]
            state[species : species + 1, part] = temp_ref[here : here + 1, :]

    def spend(group, begin):
        top, low = halves(states[group][:, begin : begin + reach])
        operand = jnp.concatenate([top, low, top], axis=0)
        return jnp.dot(gather_w[...], operand, preferred_element_type=f32)

    def react(group, begin, progress):
        heat = states[group][species : species + 1, begin : begin + reach]
        inverse = 1.0 / (1.0 + jnp.abs(heat))
        energy = jnp.concatenate([energy_b[...]] * (reach // lanes), axis=1)
        return halves(jnp.exp2(energy * inverse) * progress)

    counts = [tallies[0, tile] for tile in range(tiles)]
    turns = functools.reduce(jnp.maximum, counts)

    def per_cell(group, begin, turn):
        first = group * group_len + begin
        piece = min(tile_len, reach)
        row = []
        for cell in range(first, first + reach, piece):
            count = jnp.full((1, piece), counts[cell // tile_len], jnp.int32)
            row.append(jnp.where(turn < count, step_time / count.astype(f32), 0.0))
        return jnp.concatenate(row, axis=1)

    def back(group, begin, flux, turn):
        flux_hi, flux_lo = flux
        operand = jnp.concatenate([flux_hi[deep:], flux_lo, flux_hi[deep:]], axis=0)
        first = jnp.dot(scatter_one[...], flux_hi[:deep], preferred_element_type=f32)
        second = jnp.dot(scatter_two[...], operand, preferred_element_type=f32)
        change = (first[:used] + first[used:]) + second
        states[group][:used, begin : begin + reach] += per_cell(group, begin, turn) * change

    work = [(group, begin) for group in range(groups) for begin in range(0, group_len, reach)]

    def step(turn, carry):
        pending = (*work[-1], (late_hi[...], late_lo[...]), turn - 1)
        progress = ahead[...]
        for here, after in zip(work, work[1:] + work[:1]):
            coming = spend(*after)
            back(*pending)
            pending = (*here, react(*here, progress), turn)
            progress = coming
        ahead[...] = progress
        late_hi[...], late_lo[...] = pending[2]
        return carry

    ahead[...] = spend(*work[0])
    lax.fori_loop(0, turns, step, 0)
    back(*work[-1], (late_hi[...], late_lo[...]), turns - 1)

    lane = lax.broadcasted_iota(jnp.int32, share_out.shape, 1)
    shares = jnp.zeros(share_out.shape, f32)
    for group, state in enumerate(states):
        heat = state[species + 1 : species + 2, :]
        for k in range(group_rows):
            here = group * group_rows + k
            part = slice(k * width, (k + 1) * width)
            rhs_out[here : here + 1, :] = flow_ref[here : here + 1, :] + heat[:, part]
        squares = heat * heat
        for cell in range(0, group_len, min(tile_len, group_len)):
            tile = (group * group_len + cell) // tile_len
            total = jnp.sum(squares[:, cell : cell + tile_len], axis=1, keepdims=True)
            shares = shares + jnp.where(lane == owners[0, tile], total, 0.0)
    share_out[...] = shares


def unpack_kernel(*refs, groups):
    states = refs[:groups]
    spec_hbm, temp_out = refs[groups : groups + 2]
    blocks = refs[groups + 2 : 2 * groups + 2]
    leave = refs[2 * groups + 2]
    species = spec_hbm.shape[0]
    pad_s, group_rows, width = blocks[0].shape
    copies = []
    for group, (state, block) in enumerate(zip(states, blocks)):
        lines = block.reshape(pad_s * group_rows, width)
        for k in range(group_rows):
            here = group * group_rows + k
            part = slice(k * width, (k + 1) * width)
            lines[pl.ds(k, pad_s, stride=group_rows), :] = state[:pad_s, part]
            temp_out[here : here + 1, :] = state[species : species + 1, part]
        copy = pltpu.make_async_copy(
            block.at[:species],
            spec_hbm.at[:, group * group_rows : (group + 1) * group_rows, :],
            leave.at[group],
        )
        copy.start()
        copies.append(copy)
    for copy in copies:
        copy.wait()


def chemistry(spec, temp, flow, tallies, owners, consumed, molar, factor, energy, enthalpy):
    species, rows, width = spec.shape
    reactions = consumed.shape[0]
    group_rows = 8
    groups = rows // group_rows
    group_len = group_rows * width
    depth = round_up(species + 2, 64)
    used = round_up(species + 2, 8)
    pad_r = round_up(reactions, 16)
    deep = pad_r // 256 * 256
    reach = 256
    hbm = pl.BlockSpec(memory_space=pltpu.HBM)
    vmem = pl.BlockSpec(memory_space=pltpu.VMEM)
    block = pltpu.VMEM((round_up(species, 8), group_rows, width), f32)
    rhs, shares, *states = pl.pallas_call(
        functools.partial(chemistry_kernel, groups=groups),
        out_shape=[
            jax.ShapeDtypeStruct(temp.shape, f32),
            jax.ShapeDtypeStruct((8, width), f32),
        ]
        + [jax.ShapeDtypeStruct((depth, group_len), f32)] * groups,
        in_specs=[hbm] * 10,
        out_specs=[vmem] * (2 + groups),
        scratch_shapes=[block] * groups
        + [
            pltpu.SMEM(tallies.shape, jnp.int32),
            pltpu.SMEM(owners.shape, jnp.int32),
            pltpu.VMEM(temp.shape, f32),
            pltpu.VMEM(flow.shape, f32),
            pltpu.VMEM((species, reactions), f32),
            pltpu.VMEM((species, reactions), f32),
            pltpu.VMEM((reactions,), f32),
            pltpu.VMEM((reactions,), f32),
            pltpu.VMEM((reactions,), f32),
            pltpu.VMEM((pad_r, 3 * depth), bf16),
            pltpu.VMEM((2 * used, deep), bf16),
            pltpu.VMEM((used, 3 * pad_r - 2 * deep), bf16),
            pltpu.VMEM((pad_r, lanes), f32),
            pltpu.VMEM((lanes, round_up(reactions, lanes)), f32),
            pltpu.VMEM((pad_r, reach), bf16),
            pltpu.VMEM((pad_r, reach), bf16),
            pltpu.VMEM((pad_r, reach), f32),
            pltpu.SemaphoreType.DMA((9 + groups,)),
        ],
        compiler_params=pltpu.CompilerParams(vmem_limit_bytes=24 << 20),
        name="chemistry",
    )(
        *(
            pltpu.with_memory_space_constraint(array, pltpu.HBM)
            for array in (
                tallies,
                owners,
                spec,
                temp,
                flow,
                consumed.T,
                molar.T,
                factor,
                energy,
                enthalpy,
            )
        )
    )
    spec_new, temp_new = pl.pallas_call(
        functools.partial(unpack_kernel, groups=groups),
        out_shape=[
            jax.ShapeDtypeStruct(spec.shape, f32),
            jax.ShapeDtypeStruct(temp.shape, f32),
        ],
        in_specs=[vmem] * groups,
        out_specs=[hbm, vmem],
        scratch_shapes=[block] * groups + [pltpu.SemaphoreType.DMA((groups,))],
        compiler_params=pltpu.CompilerParams(vmem_limit_bytes=4 << 20),
        cost_estimate=pl.CostEstimate(
            flops=spec.size, bytes_accessed=8 * spec.size, transcendentals=0
        ),
        name="unpack",
    )(*states)
    return spec_new, temp_new, rhs, shares


def join_kernel(rhs_ref, share_ref, a_ref, b_ref, out_ref, *, reach):
    width = rhs_ref.shape[1]
    even = lax.axis_index("gy") % 2 == 0
    right = jnp.where(even, a_ref[...], b_ref[...])
    left = jnp.where(even, b_ref[...], a_ref[...])
    lane = lax.broadcasted_iota(jnp.int32, rhs_ref.shape, 1)
    side = jnp.where(lane < reach, right, left)
    out_ref[:, :width] = rhs_ref[...]
    out_ref[:, width:] = side
    out_ref[0:1, width:] = jnp.where(
        (lane[0:1] < reach) | (lane[0:1] >= width - reach),
        side[0:1],
        pltpu.roll(share_ref[0:1, :], reach, 1),
    )


def join_sides(rhs, shares, a, b, reach):
    rows, width = rhs.shape
    vmem = pl.BlockSpec(memory_space=pltpu.VMEM)
    return pl.pallas_call(
        functools.partial(join_kernel, reach=reach),
        out_shape=jax.ShapeDtypeStruct((rows, 2 * width), f32),
        in_specs=[vmem] * 4,
        out_specs=vmem,
        compiler_params=pltpu.CompilerParams(vmem_limit_bytes=4 << 20),
        name="join_sides",
    )(rhs, shares, a, b)


def multigrid_kernel(*refs, reach, quick, count_x, count_y):
    if quick:
        mid_ref, a_ref, b_ref, share_ref, out_ref, burden_ref = refs
    else:
        mid_ref, a_ref, b_ref, out_ref = refs
    rows = mid_ref.shape[0]
    width = mid_ref.shape[1] // 2
    at_x = lax.axis_index("gx")
    at_y = lax.axis_index("gy")
    if quick:
        own = (
            mid_ref[0:1, width:]
            + a_ref[0:1, width:]
            + b_ref[0:1, width:]
            + pltpu.roll(share_ref[0:1, :], reach, 1)
        )
        lane = lax.broadcasted_iota(jnp.int32, own.shape, 1)
        own = jnp.where(lane == at_x + reach, own, 0.0)
        burden_ref[...] = jnp.sum(own, axis=1, keepdims=True) / (rows * width)

    even = at_x % 2 == 0
    above = jnp.where(even, b_ref[...], a_ref[...])
    below = jnp.where(even, a_ref[...], b_ref[...])
    whole = jnp.concatenate([above, mid_ref[...], below], axis=0)
    wide = whole.shape[1]
    down = lax.broadcasted_iota(jnp.int32, whole.shape, 0)
    across = lax.broadcasted_iota(jnp.int32, whole.shape, 1)
    row = at_x * rows + down - rows
    column = at_y * width + jnp.where(across >= width + width // 2, across - wide, across)
    inside = (row >= 0) & (row < count_x * rows) & (column >= 0) & (column < count_y * width)
    keep = jnp.where(inside, relax / 4.0, 0.0)
    whole = jnp.where(inside, whole, 0.0)

    def beside(field, step):
        return (
            pltpu.roll(field, step, 0)
            + pltpu.roll(field, field.shape[0] - step, 0)
            + pltpu.roll(field, step, 1)
            + pltpu.roll(field, wide - step, 1)
        )

    def needed(level, lo, hi):
        step = 2**level
        if level == LEVELS - 1:
            return lo - (COARSE - 1) * step, hi + (COARSE - 1) * step
        lo, hi = needed(level + 1, *coarse_rows(level, lo, hi))
        lo, hi = lo // (2 * step) * (2 * step), round_up(hi, 2 * step)
        return lo - SWEEPS * step, hi + SWEEPS * step

    def coarse_rows(level, lo, hi):
        step = 2**level
        lo, hi = lo - SWEEPS * step, hi + SWEEPS * step
        return lo // (2 * step) * (2 * step), round_up(hi, 2 * step)

    def cut(field, base, lo, hi):
        lo = max(lo // 8 * 8, base)
        hi = min(round_up(hi, 8), base + field.shape[0])
        return field[lo - base : hi - base], lo

    def like(full, field, base):
        return full[base : base + field.shape[0]]

    def halve(field, base, step):
        odd = (like(down, field, base) & step) != 0
        tall = field.shape[0]
        field = field + jnp.where(odd, pltpu.roll(field, step, 0), pltpu.roll(field, tall - step, 0))
        odd = (like(across, field, base) & step) != 0
        field = field + jnp.where(odd, pltpu.roll(field, step, 1), pltpu.roll(field, wide - step, 1))
        return 0.25 * field

    def sweeps(field, source, base, step, count, lo, hi):
        for left in range(count, 0, -1):
            was = base
            field, base = cut(field, was, lo - left * step, hi + left * step)
            source, _ = cut(source, was, lo - left * step, hi + left * step)
            field = like(keep, field, base) * ((field + source) + beside(field, step))
        return field, base

    def vcycle(rhs, base, level, lo, hi):
        step = 2**level
        scale = 4.0**level
        source = scale * rhs
        field = like(keep, rhs, base) * source
        if level == LEVELS - 1:
            return sweeps(field, source, base, step, COARSE - 1, lo, hi)
        for _ in range(SWEEPS - 1):
            field = like(keep, rhs, base) * ((field + source) + beside(field, step))
        resid = rhs - (4.0 * field - beside(field, step)) / scale
        coarse_lo, coarse_hi = coarse_rows(level, lo, hi)
        resid, coarse_base = cut(resid, base, *needed(level + 1, coarse_lo, coarse_hi))
        resid = halve(resid, coarse_base, step)
        coarse, coarse_base = vcycle(resid, coarse_base, level + 1, coarse_lo, coarse_hi)
        coarse, coarse_base = cut(coarse, coarse_base, coarse_lo, coarse_hi)
        part = slice(coarse_base - base, coarse_base - base + coarse.shape[0])
        return sweeps(field[part] + coarse, source[part], coarse_base, step, SWEEPS, lo, hi)

    field, base = vcycle(whole, 0, 0, rows, 2 * rows)
    out_ref[...] = field[rows - base : 2 * rows - base, :width]


def multigrid(mid, a, b, shares, reach, count_x, count_y):
    rows = mid.shape[0]
    width = mid.shape[1] // 2
    quick = shares is not None
    vmem = pl.BlockSpec(memory_space=pltpu.VMEM)
    field = jax.ShapeDtypeStruct((rows, width), f32)
    return pl.pallas_call(
        functools.partial(
            multigrid_kernel, reach=reach, quick=quick, count_x=count_x, count_y=count_y
        ),
        out_shape=(field, jax.ShapeDtypeStruct((1, 1), f32)) if quick else field,
        in_specs=[vmem] * (4 if quick else 3),
        out_specs=(vmem, vmem) if quick else vmem,
        compiler_params=pltpu.CompilerParams(vmem_limit_bytes=8 << 20),
        name="multigrid",
    )(*((mid, a, b, shares) if quick else (mid, a, b)))


def paired(axis, first, wrap=False):
    count = lax.axis_size(axis)
    pairs = []
    for low in range(first, count + first, 2):
        one, other = low % count, (low + 1) % count
        if one < other or wrap:
            pairs += [(one, other), (other, one)]
    return pairs


def shards(
    chemical_concentration,
    thermal_scaled,
    tentative_flow_spread,
    substep_numbers,
    patch_holder_lookup,
    consumed_weighting,
    molar_coefficient,
    frequency_factor_log,
    arrhenius_energy,
    enthalpy_released,
):
    count_x, count_y = lax.axis_size("gx"), lax.axis_size("gy")
    rows, width = thermal_scaled.shape
    spec_new, temp_new, rhs, shares = chemistry(
        chemical_concentration,
        thermal_scaled,
        tentative_flow_spread,
        substep_numbers,
        patch_holder_lookup,
        consumed_weighting,
        molar_coefficient,
        frequency_factor_log,
        arrhenius_energy,
        enthalpy_released,
    )
    reach = 32
    quick = count_x == 4
    far = None
    if quick:
        far = lax.ppermute(shares, "gx", [(i, i ^ 2) for i in range(4)])
    side_a = lax.ppermute(rhs, "gy", paired("gy", 0))
    side_b = lax.ppermute(rhs, "gy", paired("gy", 1))
    band = join_sides(rhs, shares, side_a, side_b, reach)
    band_a = lax.ppermute(band, "gx", paired("gx", 0))
    band_b = lax.ppermute(band, "gx", paired("gx", 1, wrap=quick))
    if quick:
        field, burden = multigrid(band, band_a, band_b, far, reach, count_x, count_y)
    else:
        field = multigrid(band, band_a, band_b, None, reach, count_x, count_y)
        burden = lax.psum_scatter(
            shares[0, :count_x], "gx", scatter_dimension=0, tiled=True
        ).reshape(1, 1) / (rows * width)
    return spec_new, temp_new, field, burden


def solution(mesh):
    return jax.shard_map(
        shards,
        mesh=mesh,
        in_specs=(
            P(None, "gx", "gy"),
            P("gx", "gy"),
            P("gx", "gy"),
            P("gx", "gy"),
            P("gx", "gy"),
            P(),
            P(),
            P(),
            P(),
            P(),
        ),
        out_specs=(P(None, "gx", "gy"), P("gx", "gy"), P("gx", "gy"), P("gx", "gy")),
        check_vma=False,
    )
```

```python
import functools
import math

import jax
import jax.numpy as jnp
from jax import lax
from jax.experimental import pallas as pl
from jax.experimental.pallas import tpu as pltpu
from jax.sharding import PartitionSpec as P


LEVELS = 3
SWEEPS = 2
COARSE = 4

step_time = 0.4
relax = 0.8
lanes = 128
log2e = math.log2(math.e)
f32 = jnp.float32
bf16 = jnp.bfloat16


def round_up(value, multiple):
    return -(-value // multiple) * multiple


def halves(value):
    top = value.astype(bf16)
    return top, (value - top.astype(f32)).astype(bf16)


def chemistry_kernel(
    tallies_hbm,
    owners_hbm,
    spec_hbm,
    temp_hbm,
    flow_hbm,
    consumed_hbm,
    molar_hbm,
    factor_hbm,
    energy_hbm,
    enthalpy_hbm,
    rhs_out,
    share_out,
    *rest,
    groups,
):
    states = rest[:groups]
    blocks = rest[groups : 2 * groups]
    (
        tallies,
        owners,
        temp_ref,
        flow_ref,
        consumed_ref,
        molar_ref,
        factor_ref,
        energy_ref,
        enthalpy_ref,
        gather_w,
        scatter_one,
        scatter_two,
        energy_b,
        staging,
        late_hi,
        late_lo,
        ahead,
        arrival,
    ) = rest[2 * groups :]
    species = spec_hbm.shape[0]
    reactions = consumed_ref.shape[1]
    depth, group_len = states[0].shape
    pad_s, group_rows, width = blocks[0].shape
    tiles = tallies.shape[1]
    tile_len = groups * group_len // tiles
    pad_r, reach = gather_w.shape[0], late_hi.shape[1]
    used = scatter_two.shape[0]
    spread = staging.shape[1]
    deep = scatter_one.shape[1]

    small = [
        (consumed_hbm, consumed_ref),
        (factor_hbm, factor_ref),
        (energy_hbm, energy_ref),
        (molar_hbm, molar_ref),
        (enthalpy_hbm, enthalpy_ref),
        (tallies_hbm, tallies),
        (owners_hbm, owners),
        (temp_hbm, temp_ref),
        (flow_hbm, flow_ref),
    ]
    small = [
        pltpu.make_async_copy(source, target, arrival.at[k])
        for k, (source, target) in enumerate(small)
    ]
    large = [
        pltpu.make_async_copy(
            spec_hbm.at[:, group * group_rows : (group + 1) * group_rows, :],
            block.at[:species],
            arrival.at[len(small) + group],
        )
        for group, block in enumerate(blocks)
    ]
    for copy in small + large:
        copy.start()

    def flat(ref):
        return jnp.pad(ref[...].reshape(1, reactions), ((0, 0), (0, spread - reactions)))

    staging[...] = jnp.zeros_like(staging)
    for copy in small:
        copy.wait()
    staging[:species, :reactions] = consumed_ref[...]
    weights = staging[...] * jnp.exp(flat(factor_ref))
    row = lax.broadcasted_iota(jnp.int32, weights.shape, 0)
    weights = jnp.where(row == species, flat(energy_ref) * -log2e, weights)
    columns = jnp.transpose(weights)[:pad_r]
    energy_b[...] = jnp.broadcast_to(columns[:, species : species + 1], energy_b.shape)
    lane = lax.broadcasted_iota(jnp.int32, columns.shape, 1)
    top, low = halves(jnp.where(lane < species, columns, 0.0)[:, :depth])
    gather_w[...] = jnp.concatenate([top, top, low], axis=1)
    staging[:species, :reactions] = molar_ref[...]
    enthalpy = flat(enthalpy_ref)
    weights = jnp.where((row == species) | (row == species + 1), enthalpy, staging[...])[:used]
    top = weights.astype(bf16).astype(f32)
    low = (weights - top)[:, :pad_r]
    top = top[:, :pad_r]
    scatter_one[...] = jnp.concatenate([top[:, :deep], low[:, :deep]], axis=0).astype(bf16)
    scatter_two[...] = jnp.concatenate([top[:, deep:], top, low[:, deep:]], axis=1).astype(bf16)

    def load(group):
        state, block = states[group], blocks[group]
        lines = block.reshape(pad_s * group_rows, width)
        state[species:, :] = jnp.zeros((depth - species, group_len), f32)
        for k in range(group_rows):
            here = group * group_rows + k
            part = slice(k * width, (k + 1) * width)
            state[:species, part] = lines[pl.ds(k, species, stride=group_rows), :]
            state[species : species + 1, part] = temp_ref[here : here + 1, :]

    def spend(group, begin):
        top, low = halves(states[group][:, begin : begin + reach])
        operand = jnp.concatenate([top, low, top], axis=0)
        return jnp.dot(gather_w[...], operand, preferred_element_type=f32)

    def react(group, begin, progress):
        heat = states[group][species : species + 1, begin : begin + reach]
        inverse = 1.0 / (1.0 + jnp.abs(heat))
        energy = jnp.concatenate([energy_b[...]] * (reach // lanes), axis=1)
        return halves(jnp.exp2(energy * inverse) * progress)

    counts = [tallies[0, tile] for tile in range(tiles)]
    turns = functools.reduce(jnp.maximum, counts)

    def per_cell(group, begin, turn):
        first = group * group_len + begin
        piece = min(tile_len, reach)
        row = []
        for cell in range(first, first + reach, piece):
            count = jnp.full((1, piece), counts[cell // tile_len], jnp.int32)
            row.append(jnp.where(turn < count, step_time / count.astype(f32), 0.0))
        return jnp.concatenate(row, axis=1)

    def back(group, begin, flux, turn):
        flux_hi, flux_lo = flux
        operand = jnp.concatenate([flux_hi[deep:], flux_lo, flux_hi[deep:]], axis=0)
        first = jnp.dot(scatter_one[...], flux_hi[:deep], preferred_element_type=f32)
        second = jnp.dot(scatter_two[...], operand, preferred_element_type=f32)
        change = (first[:used] + first[used:]) + second
        states[group][:used, begin : begin + reach] += per_cell(group, begin, turn) * change

    work = [(group, begin) for group in range(groups) for begin in range(0, group_len, reach)]

    def step(turn, pending, progress, arrive):
        for here, after in zip(work, work[1:] + work[:1]):
            arrive(*after)
            coming = spend(*after)
            if pending is not None:
                back(*pending)
            pending = (*here, react(*here, progress), turn)
            progress = coming
        ahead[...] = progress
        late_hi[...], late_lo[...] = pending[2]

    def first_seen(group, begin):
        if begin == 0 and group > 0:
            load(group)

    def again(turn, carry):
        pending = (*work[-1], (late_hi[...], late_lo[...]), turn - 1)
        step(turn, pending, ahead[...], lambda group, begin: None)
        return carry

    for copy in large:
        copy.wait()
    load(0)
    step(0, None, spend(*work[0]), first_seen)
    lax.fori_loop(1, turns, again, 0)
    back(*work[-1], (late_hi[...], late_lo[...]), turns - 1)

    lane = lax.broadcasted_iota(jnp.int32, share_out.shape, 1)
    shares = jnp.zeros(share_out.shape, f32)
    for group, state in enumerate(states):
        heat = state[species + 1 : species + 2, :]
        for k in range(group_rows):
            here = group * group_rows + k
            part = slice(k * width, (k + 1) * width)
            rhs_out[here : here + 1, :] = flow_ref[here : here + 1, :] + heat[:, part]
        squares = heat * heat
        for cell in range(0, group_len, min(tile_len, group_len)):
            tile = (group * group_len + cell) // tile_len
            total = jnp.sum(squares[:, cell : cell + tile_len], axis=1, keepdims=True)
            shares = shares + jnp.where(lane == owners[0, tile], total, 0.0)
    share_out[...] = shares


def unpack_kernel(*refs, groups):
    states = refs[:groups]
    spec_hbm, temp_out = refs[groups : groups + 2]
    blocks = refs[groups + 2 : 2 * groups + 2]
    leave = refs[2 * groups + 2]
    species = spec_hbm.shape[0]
    pad_s, group_rows, width = blocks[0].shape
    copies = []
    for group, (state, block) in enumerate(zip(states, blocks)):
        lines = block.reshape(pad_s * group_rows, width)
        for k in range(group_rows):
            here = group * group_rows + k
            part = slice(k * width, (k + 1) * width)
            lines[pl.ds(k, pad_s, stride=group_rows), :] = state[:pad_s, part]
            temp_out[here : here + 1, :] = state[species : species + 1, part]
        copy = pltpu.make_async_copy(
            block.at[:species],
            spec_hbm.at[:, group * group_rows : (group + 1) * group_rows, :],
            leave.at[group],
        )
        copy.start()
        copies.append(copy)
    for copy in copies:
        copy.wait()


def chemistry(spec, temp, flow, tallies, owners, consumed, molar, factor, energy, enthalpy):
    species, rows, width = spec.shape
    reactions = consumed.shape[0]
    group_rows = 8
    groups = rows // group_rows
    group_len = group_rows * width
    depth = round_up(species + 2, 64)
    used = round_up(species + 2, 8)
    pad_r = round_up(reactions, 16)
    deep = pad_r // 256 * 256
    reach = 256
    hbm = pl.BlockSpec(memory_space=pltpu.HBM)
    vmem = pl.BlockSpec(memory_space=pltpu.VMEM)
    block = pltpu.VMEM((round_up(species, 8), group_rows, width), f32)
    rhs, shares, *states = pl.pallas_call(
        functools.partial(chemistry_kernel, groups=groups),
        out_shape=[
            jax.ShapeDtypeStruct(temp.shape, f32),
            jax.ShapeDtypeStruct((8, width), f32),
        ]
        + [jax.ShapeDtypeStruct((depth, group_len), f32)] * groups,
        in_specs=[hbm] * 10,
        out_specs=[vmem] * (2 + groups),
        scratch_shapes=[block] * groups
        + [
            pltpu.SMEM(tallies.shape, jnp.int32),
            pltpu.SMEM(owners.shape, jnp.int32),
            pltpu.VMEM(temp.shape, f32),
            pltpu.VMEM(flow.shape, f32),
            pltpu.VMEM((species, reactions), f32),
            pltpu.VMEM((species, reactions), f32),
            pltpu.VMEM((reactions,), f32),
            pltpu.VMEM((reactions,), f32),
            pltpu.VMEM((reactions,), f32),
            pltpu.VMEM((pad_r, 3 * depth), bf16),
            pltpu.VMEM((2 * used, deep), bf16),
            pltpu.VMEM((used, 3 * pad_r - 2 * deep), bf16),
            pltpu.VMEM((pad_r, lanes), f32),
            pltpu.VMEM((lanes, round_up(reactions, lanes)), f32),
            pltpu.VMEM((pad_r, reach), bf16),
            pltpu.VMEM((pad_r, reach), bf16),
            pltpu.VMEM((pad_r, reach), f32),
            pltpu.SemaphoreType.DMA((9 + groups,)),
        ],
        compiler_params=pltpu.CompilerParams(vmem_limit_bytes=24 << 20),
        name="chemistry",
    )(
        *(
            pltpu.with_memory_space_constraint(array, pltpu.HBM)
            for array in (
                tallies,
                owners,
                spec,
                temp,
                flow,
                consumed.T,
                molar.T,
                factor,
                energy,
                enthalpy,
            )
        )
    )
    spec_new, temp_new = pl.pallas_call(
        functools.partial(unpack_kernel, groups=groups),
        out_shape=[
            jax.ShapeDtypeStruct(spec.shape, f32),
            jax.ShapeDtypeStruct(temp.shape, f32),
        ],
        in_specs=[vmem] * groups,
        out_specs=[hbm, vmem],
        scratch_shapes=[block] * groups + [pltpu.SemaphoreType.DMA((groups,))],
        compiler_params=pltpu.CompilerParams(vmem_limit_bytes=4 << 20),
        cost_estimate=pl.CostEstimate(
            flops=spec.size, bytes_accessed=8 * spec.size, transcendentals=0
        ),
        name="unpack",
    )(*states)
    return spec_new, temp_new, rhs, shares


def join_kernel(rhs_ref, share_ref, a_ref, b_ref, out_ref, *, reach):
    width = rhs_ref.shape[1]
    even = lax.axis_index("gy") % 2 == 0
    right = jnp.where(even, a_ref[...], b_ref[...])
    left = jnp.where(even, b_ref[...], a_ref[...])
    lane = lax.broadcasted_iota(jnp.int32, rhs_ref.shape, 1)
    side = jnp.where(lane < reach, right, left)
    out_ref[:, :width] = rhs_ref[...]
    out_ref[:, width:] = side
    out_ref[0:1, width:] = jnp.where(
        (lane[0:1] < reach) | (lane[0:1] >= width - reach),
        side[0:1],
        pltpu.roll(share_ref[0:1, :], reach, 1),
    )


def join_sides(rhs, shares, a, b, reach):
    rows, width = rhs.shape
    vmem = pl.BlockSpec(memory_space=pltpu.VMEM)
    return pl.pallas_call(
        functools.partial(join_kernel, reach=reach),
        out_shape=jax.ShapeDtypeStruct((rows, 2 * width), f32),
        in_specs=[vmem] * 4,
        out_specs=vmem,
        compiler_params=pltpu.CompilerParams(vmem_limit_bytes=4 << 20),
        name="join_sides",
    )(rhs, shares, a, b)


def multigrid_kernel(*refs, reach, quick, count_x, count_y):
    if quick:
        mid_ref, a_ref, b_ref, share_ref, out_ref, burden_ref = refs
    else:
        mid_ref, a_ref, b_ref, out_ref = refs
    rows = mid_ref.shape[0]
    width = mid_ref.shape[1] // 2
    at_x = lax.axis_index("gx")
    at_y = lax.axis_index("gy")
    if quick:
        own = (
            mid_ref[0:1, width:]
            + a_ref[0:1, width:]
            + b_ref[0:1, width:]
            + pltpu.roll(share_ref[0:1, :], reach, 1)
        )
        lane = lax.broadcasted_iota(jnp.int32, own.shape, 1)
        own = jnp.where(lane == at_x + reach, own, 0.0)
        burden_ref[...] = jnp.sum(own, axis=1, keepdims=True) / (rows * width)

    even = at_x % 2 == 0
    above = jnp.where(even, b_ref[...], a_ref[...])
    below = jnp.where(even, a_ref[...], b_ref[...])
    whole = jnp.concatenate([above, mid_ref[...], below], axis=0)
    wide = whole.shape[1]
    down = lax.broadcasted_iota(jnp.int32, whole.shape, 0)
    across = lax.broadcasted_iota(jnp.int32, whole.shape, 1)
    row = at_x * rows + down - rows
    column = at_y * width + jnp.where(across >= width + width // 2, across - wide, across)
    inside = (row >= 0) & (row < count_x * rows) & (column >= 0) & (column < count_y * width)
    keep = jnp.where(inside, relax / 4.0, 0.0)
    whole = jnp.where(inside, whole, 0.0)

    def beside(field, step):
        return (
            pltpu.roll(field, step, 0)
            + pltpu.roll(field, field.shape[0] - step, 0)
            + pltpu.roll(field, step, 1)
            + pltpu.roll(field, wide - step, 1)
        )

    def needed(level, lo, hi):
        step = 2**level
        if level == LEVELS - 1:
            return lo - (COARSE - 1) * step, hi + (COARSE - 1) * step
        lo, hi = needed(level + 1, *coarse_rows(level, lo, hi))
        lo, hi = lo // (2 * step) * (2 * step), round_up(hi, 2 * step)
        return lo - SWEEPS * step, hi + SWEEPS * step

    def coarse_rows(level, lo, hi):
        step = 2**level
        lo, hi = lo - SWEEPS * step, hi + SWEEPS * step
        return lo // (2 * step) * (2 * step), round_up(hi, 2 * step)

    def cut(field, base, lo, hi):
        lo = max(lo // 8 * 8, base)
        hi = min(round_up(hi, 8), base + field.shape[0])
        return field[lo - base : hi - base], lo

    def like(full, field, base):
        return full[base : base + field.shape[0]]

    def halve(field, base, step):
        odd = (like(down, field, base) & step) != 0
        tall = field.shape[0]
        field = field + jnp.where(odd, pltpu.roll(field, step, 0), pltpu.roll(field, tall - step, 0))
        odd = (like(across, field, base) & step) != 0
        field = field + jnp.where(odd, pltpu.roll(field, step, 1), pltpu.roll(field, wide - step, 1))
        return 0.25 * field

    def sweeps(field, source, base, step, count, lo, hi):
        for left in range(count, 0, -1):
            was = base
            field, base = cut(field, was, lo - left * step, hi + left * step)
            source, _ = cut(source, was, lo - left * step, hi + left * step)
            field = like(keep, field, base) * ((field + source) + beside(field, step))
        return field, base

    def vcycle(rhs, base, level, lo, hi):
        step = 2**level
        scale = 4.0**level
        source = scale * rhs
        field = like(keep, rhs, base) * source
        if level == LEVELS - 1:
            return sweeps(field, source, base, step, COARSE - 1, lo, hi)
        for _ in range(SWEEPS - 1):
            field = like(keep, rhs, base) * ((field + source) + beside(field, step))
        resid = rhs - (4.0 * field - beside(field, step)) / scale
        coarse_lo, coarse_hi = coarse_rows(level, lo, hi)
        resid, coarse_base = cut(resid, base, *needed(level + 1, coarse_lo, coarse_hi))
        resid = halve(resid, coarse_base, step)
        coarse, coarse_base = vcycle(resid, coarse_base, level + 1, coarse_lo, coarse_hi)
        coarse, coarse_base = cut(coarse, coarse_base, coarse_lo, coarse_hi)
        part = slice(coarse_base - base, coarse_base - base + coarse.shape[0])
        return sweeps(field[part] + coarse, source[part], coarse_base, step, SWEEPS, lo, hi)

    field, base = vcycle(whole, 0, 0, rows, 2 * rows)
    out_ref[...] = field[rows - base : 2 * rows - base, :width]


def multigrid(mid, a, b, shares, reach, count_x, count_y):
    rows = mid.shape[0]
    width = mid.shape[1] // 2
    quick = shares is not None
    vmem = pl.BlockSpec(memory_space=pltpu.VMEM)
    field = jax.ShapeDtypeStruct((rows, width), f32)
    return pl.pallas_call(
        functools.partial(
            multigrid_kernel, reach=reach, quick=quick, count_x=count_x, count_y=count_y
        ),
        out_shape=(field, jax.ShapeDtypeStruct((1, 1), f32)) if quick else field,
        in_specs=[vmem] * (4 if quick else 3),
        out_specs=(vmem, vmem) if quick else vmem,
        compiler_params=pltpu.CompilerParams(vmem_limit_bytes=8 << 20),
        name="multigrid",
    )(*((mid, a, b, shares) if quick else (mid, a, b)))


def paired(axis, first, wrap=False):
    count = lax.axis_size(axis)
    pairs = []
    for low in range(first, count + first, 2):
        one, other = low % count, (low + 1) % count
        if one < other or wrap:
            pairs += [(one, other), (other, one)]
    return pairs


def shards(
    chemical_concentration,
    thermal_scaled,
    tentative_flow_spread,
    substep_numbers,
    patch_holder_lookup,
    consumed_weighting,
    molar_coefficient,
    frequency_factor_log,
    arrhenius_energy,
    enthalpy_released,
):
    count_x, count_y = lax.axis_size("gx"), lax.axis_size("gy")
    rows, width = thermal_scaled.shape
    spec_new, temp_new, rhs, shares = chemistry(
        chemical_concentration,
        thermal_scaled,
        tentative_flow_spread,
        substep_numbers,
        patch_holder_lookup,
        consumed_weighting,
        molar_coefficient,
        frequency_factor_log,
        arrhenius_energy,
        enthalpy_released,
    )
    reach = 32
    quick = count_x == 4
    far = None
    if quick:
        far = lax.ppermute(shares, "gx", [(i, i ^ 2) for i in range(4)])
    side_a = lax.ppermute(rhs, "gy", paired("gy", 0))
    side_b = lax.ppermute(rhs, "gy", paired("gy", 1))
    band = join_sides(rhs, shares, side_a, side_b, reach)
    band_a = lax.ppermute(band, "gx", paired("gx", 0))
    band_b = lax.ppermute(band, "gx", paired("gx", 1, wrap=quick))
    if quick:
        field, burden = multigrid(band, band_a, band_b, far, reach, count_x, count_y)
    else:
        field = multigrid(band, band_a, band_b, None, reach, count_x, count_y)
        burden = lax.psum_scatter(
            shares[0, :count_x], "gx", scatter_dimension=0, tiled=True
        ).reshape(1, 1) / (rows * width)
    return spec_new, temp_new, field, burden


def solution(mesh):
    return jax.shard_map(
        shards,
        mesh=mesh,
        in_specs=(
            P(None, "gx", "gy"),
            P("gx", "gy"),
            P("gx", "gy"),
            P("gx", "gy"),
            P("gx", "gy"),
            P(),
            P(),
            P(),
            P(),
            P(),
        ),
        out_specs=(P(None, "gx", "gy"), P("gx", "gy"), P("gx", "gy"), P("gx", "gy")),
        check_vma=False,
    )
```

```python
import functools
import math

import jax
import jax.numpy as jnp
from jax import lax
from jax.experimental import pallas as pl
from jax.experimental.pallas import tpu as pltpu
from jax.sharding import PartitionSpec as P


LEVELS = 3
SWEEPS = 2
COARSE = 4

step_time = 0.4
relax = 0.8
lanes = 128
log2e = math.log2(math.e)
f32 = jnp.float32
bf16 = jnp.bfloat16


def round_up(value, multiple):
    return -(-value // multiple) * multiple


def halves(value):
    top = value.astype(bf16)
    return top, (value - top.astype(f32)).astype(bf16)


def chemistry_kernel(
    tallies_hbm,
    owners_hbm,
    spec_hbm,
    temp_hbm,
    flow_hbm,
    consumed_hbm,
    molar_hbm,
    factor_hbm,
    energy_hbm,
    enthalpy_hbm,
    rhs_out,
    share_out,
    *rest,
    groups,
):
    states = rest[:groups]
    blocks = rest[groups : 2 * groups]
    (
        tallies,
        owners,
        temp_ref,
        flow_ref,
        consumed_ref,
        molar_ref,
        factor_ref,
        energy_ref,
        enthalpy_ref,
        gather_w,
        scatter_one,
        scatter_two,
        energy_b,
        staging,
        late_hi,
        late_lo,
        ahead,
        arrival,
    ) = rest[2 * groups :]
    species = spec_hbm.shape[0]
    reactions = consumed_ref.shape[1]
    depth, group_len = states[0].shape
    pad_s, group_rows, width = blocks[0].shape
    tiles = tallies.shape[1]
    tile_len = groups * group_len // tiles
    pad_r, reach = gather_w.shape[0], late_hi.shape[1]
    used = scatter_two.shape[0]
    spread = staging.shape[1]
    deep = scatter_one.shape[1]

    small = [
        (consumed_hbm, consumed_ref),
        (factor_hbm, factor_ref),
        (energy_hbm, energy_ref),
        (molar_hbm, molar_ref),
        (enthalpy_hbm, enthalpy_ref),
        (tallies_hbm, tallies),
        (owners_hbm, owners),
        (temp_hbm, temp_ref),
        (flow_hbm, flow_ref),
    ]
    small = [
        pltpu.make_async_copy(source, target, arrival.at[k])
        for k, (source, target) in enumerate(small)
    ]
    large = [
        pltpu.make_async_copy(
            spec_hbm.at[:, group * group_rows : (group + 1) * group_rows, :],
            block.at[:species],
            arrival.at[len(small) + group],
        )
        for group, block in enumerate(blocks)
    ]
    for copy in small + large:
        copy.start()

    def flat(ref):
        return jnp.pad(ref[...].reshape(1, reactions), ((0, 0), (0, spread - reactions)))

    staging[...] = jnp.zeros_like(staging)
    late_hi[...] = jnp.zeros_like(late_hi)
    late_lo[...] = jnp.zeros_like(late_lo)
    for copy in small:
        copy.wait()
    staging[:species, :reactions] = consumed_ref[...]
    weights = staging[...] * jnp.exp(flat(factor_ref))
    row = lax.broadcasted_iota(jnp.int32, weights.shape, 0)
    weights = jnp.where(row == species, flat(energy_ref) * -log2e, weights)
    columns = jnp.transpose(weights)[:pad_r]
    energy_b[...] = jnp.broadcast_to(columns[:, species : species + 1], energy_b.shape)
    lane = lax.broadcasted_iota(jnp.int32, columns.shape, 1)
    top, low = halves(jnp.where(lane < species, columns, 0.0)[:, :depth])
    gather_w[...] = jnp.concatenate([top, top, low], axis=1)
    staging[:species, :reactions] = molar_ref[...]
    enthalpy = flat(enthalpy_ref)
    weights = jnp.where((row == species) | (row == species + 1), enthalpy, staging[...])[:used]
    top = weights.astype(bf16).astype(f32)
    low = (weights - top)[:, :pad_r]
    top = top[:, :pad_r]
    scatter_one[...] = jnp.concatenate([top[:, :deep], low[:, :deep]], axis=0).astype(bf16)
    scatter_two[...] = jnp.concatenate([top[:, deep:], top, low[:, deep:]], axis=1).astype(bf16)

    for group, (state, block) in enumerate(zip(states, blocks)):
        large[group].wait()
        lines = block.reshape(pad_s * group_rows, width)
        state[species:, :] = jnp.zeros((depth - species, group_len), f32)
        for k in range(group_rows):
            here = group * group_rows + k
            part = slice(k * width, (k + 1) * width)
            state[:species, part] = lines[pl.ds(k, species, stride=group_rows), :]
            state[species : species + 1, part] = temp_ref[here : here + 1, :]

    def spend(group, begin):
        top, low = halves(states[group][:, begin : begin + reach])
        operand = jnp.concatenate([top, low, top], axis=0)
        return jnp.dot(gather_w[...], operand, preferred_element_type=f32)

    def react(group, begin, progress):
        heat = states[group][species : species + 1, begin : begin + reach]
        inverse = 1.0 / (1.0 + jnp.abs(heat))
        energy = jnp.concatenate([energy_b[...]] * (reach // lanes), axis=1)
        return halves(jnp.exp2(energy * inverse) * progress)

    counts = [tallies[0, tile] for tile in range(tiles)]
    turns = functools.reduce(jnp.maximum, counts)

    def per_cell(group, begin, turn):
        first = group * group_len + begin
        piece = min(tile_len, reach)
        row = []
        for cell in range(first, first + reach, piece):
            count = jnp.full((1, piece), counts[cell // tile_len], jnp.int32)
            row.append(jnp.where(turn < count, step_time / count.astype(f32), 0.0))
        return jnp.concatenate(row, axis=1)

    def back(group, begin, flux, turn):
        flux_hi, flux_lo = flux
        operand = jnp.concatenate([flux_hi[deep:], flux_lo, flux_hi[deep:]], axis=0)
        first = jnp.dot(scatter_one[...], flux_hi[:deep], preferred_element_type=f32)
        second = jnp.dot(scatter_two[...], operand, preferred_element_type=f32)
        change = (first[:used] + first[used:]) + second
        states[group][:used, begin : begin + reach] += per_cell(group, begin, turn) * change

    work = [(group, begin) for group in range(groups) for begin in range(0, group_len, reach)]

    def step(turn, carry):
        pending = (*work[-1], (late_hi[...], late_lo[...]), turn - 1)
        progress = ahead[...]
        for here, after in zip(work, work[1:] + work[:1]):
            coming = spend(*after)
            back(*pending)
            pending = (*here, react(*here, progress), turn)
            progress = coming
        ahead[...] = progress
        late_hi[...], late_lo[...] = pending[2]
        return carry

    ahead[...] = spend(*work[0])
    lax.fori_loop(0, turns, step, 0)
    back(*work[-1], (late_hi[...], late_lo[...]), turns - 1)

    lane = lax.broadcasted_iota(jnp.int32, share_out.shape, 1)
    shares = jnp.zeros(share_out.shape, f32)
    for group, state in enumerate(states):
        heat = state[species + 1 : species + 2, :]
        for k in range(group_rows):
            here = group * group_rows + k
            part = slice(k * width, (k + 1) * width)
            rhs_out[here : here + 1, :] = flow_ref[here : here + 1, :] + heat[:, part]
        squares = heat * heat
        for cell in range(0, group_len, min(tile_len, group_len)):
            tile = (group * group_len + cell) // tile_len
            total = jnp.sum(squares[:, cell : cell + tile_len], axis=1, keepdims=True)
            shares = shares + jnp.where(lane == owners[0, tile], total, 0.0)
    share_out[...] = shares


def unpack_kernel(*refs, groups):
    states = refs[:groups]
    spec_hbm, temp_out = refs[groups : groups + 2]
    blocks = refs[groups + 2 : 2 * groups + 2]
    leave = refs[2 * groups + 2]
    species = spec_hbm.shape[0]
    pad_s, group_rows, width = blocks[0].shape
    copies = []
    for group, (state, block) in enumerate(zip(states, blocks)):
        lines = block.reshape(pad_s * group_rows, width)
        for k in range(group_rows):
            here = group * group_rows + k
            part = slice(k * width, (k + 1) * width)
            lines[pl.ds(k, pad_s, stride=group_rows), :] = state[:pad_s, part]
            temp_out[here : here + 1, :] = state[species : species + 1, part]
        copy = pltpu.make_async_copy(
            block.at[:species],
            spec_hbm.at[:, group * group_rows : (group + 1) * group_rows, :],
            leave.at[group],
        )
        copy.start()
        copies.append(copy)
    for copy in copies:
        copy.wait()


def chemistry(spec, temp, flow, tallies, owners, consumed, molar, factor, energy, enthalpy):
    species, rows, width = spec.shape
    reactions = consumed.shape[0]
    group_rows = 8
    groups = rows // group_rows
    group_len = group_rows * width
    depth = round_up(species + 2, 64)
    used = round_up(species + 2, 8)
    pad_r = round_up(reactions, 16)
    deep = pad_r // 256 * 256
    reach = 256
    hbm = pl.BlockSpec(memory_space=pltpu.HBM)
    vmem = pl.BlockSpec(memory_space=pltpu.VMEM)
    block = pltpu.VMEM((round_up(species, 8), group_rows, width), f32)
    rhs, shares, *states = pl.pallas_call(
        functools.partial(chemistry_kernel, groups=groups),
        out_shape=[
            jax.ShapeDtypeStruct(temp.shape, f32),
            jax.ShapeDtypeStruct((8, width), f32),
        ]
        + [jax.ShapeDtypeStruct((depth, group_len), f32)] * groups,
        in_specs=[hbm] * 10,
        out_specs=[vmem] * (2 + groups),
        scratch_shapes=[block] * groups
        + [
            pltpu.SMEM(tallies.shape, jnp.int32),
            pltpu.SMEM(owners.shape, jnp.int32),
            pltpu.VMEM(temp.shape, f32),
            pltpu.VMEM(flow.shape, f32),
            pltpu.VMEM((species, reactions), f32),
            pltpu.VMEM((species, reactions), f32),
            pltpu.VMEM((reactions,), f32),
            pltpu.VMEM((reactions,), f32),
            pltpu.VMEM((reactions,), f32),
            pltpu.VMEM((pad_r, 3 * depth), bf16),
            pltpu.VMEM((2 * used, deep), bf16),
            pltpu.VMEM((used, 3 * pad_r - 2 * deep), bf16),
            pltpu.VMEM((pad_r, lanes), f32),
            pltpu.VMEM((lanes, round_up(reactions, lanes)), f32),
            pltpu.VMEM((pad_r, reach), bf16),
            pltpu.VMEM((pad_r, reach), bf16),
            pltpu.VMEM((pad_r, reach), f32),
            pltpu.SemaphoreType.DMA((9 + groups,)),
        ],
        compiler_params=pltpu.CompilerParams(vmem_limit_bytes=24 << 20),
        name="chemistry",
    )(
        *(
            pltpu.with_memory_space_constraint(array, pltpu.HBM)
            for array in (
                tallies,
                owners,
                spec,
                temp,
                flow,
                consumed.T,
                molar.T,
                factor,
                energy,
                enthalpy,
            )
        )
    )
    outputs = unpack(spec, temp, states, groups, block)
    return *outputs, rhs, shares


def unpack(spec, temp, states, groups, block):
    hbm = pl.BlockSpec(memory_space=pltpu.HBM)
    vmem = pl.BlockSpec(memory_space=pltpu.VMEM)
    return pl.pallas_call(
        functools.partial(unpack_kernel, groups=groups),
        out_shape=[
            jax.ShapeDtypeStruct(spec.shape, f32),
            jax.ShapeDtypeStruct(temp.shape, f32),
        ],
        in_specs=[vmem] * groups,
        out_specs=[hbm, vmem],
        scratch_shapes=[block] * groups + [pltpu.SemaphoreType.DMA((groups,))],
        compiler_params=pltpu.CompilerParams(vmem_limit_bytes=4 << 20),
        cost_estimate=pl.CostEstimate(
            flops=spec.size, bytes_accessed=8 * spec.size, transcendentals=0
        ),
        name="unpack",
    )(*states)


def join_kernel(rhs_ref, share_ref, a_ref, b_ref, out_ref, *, reach):
    width = rhs_ref.shape[1]
    even = lax.axis_index("gy") % 2 == 0
    right = jnp.where(even, a_ref[...], b_ref[...])
    left = jnp.where(even, b_ref[...], a_ref[...])
    lane = lax.broadcasted_iota(jnp.int32, rhs_ref.shape, 1)
    side = jnp.where(lane < reach, right, left)
    out_ref[:, :width] = rhs_ref[...]
    out_ref[:, width:] = side
    out_ref[0:1, width:] = jnp.where(
        (lane[0:1] < reach) | (lane[0:1] >= width - reach),
        side[0:1],
        pltpu.roll(share_ref[0:1, :], reach, 1),
    )


def join_sides(rhs, shares, a, b, reach):
    rows, width = rhs.shape
    vmem = pl.BlockSpec(memory_space=pltpu.VMEM)
    return pl.pallas_call(
        functools.partial(join_kernel, reach=reach),
        out_shape=jax.ShapeDtypeStruct((rows, 2 * width), f32),
        in_specs=[vmem] * 4,
        out_specs=vmem,
        compiler_params=pltpu.CompilerParams(vmem_limit_bytes=4 << 20),
        name="join_sides",
    )(rhs, shares, a, b)


def multigrid_kernel(*refs, reach, quick, count_x, count_y):
    if quick:
        mid_ref, a_ref, b_ref, share_ref, out_ref, burden_ref = refs
    else:
        mid_ref, a_ref, b_ref, out_ref = refs
    rows = mid_ref.shape[0]
    width = mid_ref.shape[1] // 2
    at_x = lax.axis_index("gx")
    at_y = lax.axis_index("gy")
    if quick:
        own = (
            mid_ref[0:1, width:]
            + a_ref[0:1, width:]
            + b_ref[0:1, width:]
            + pltpu.roll(share_ref[0:1, :], reach, 1)
        )
        lane = lax.broadcasted_iota(jnp.int32, own.shape, 1)
        own = jnp.where(lane == at_x + reach, own, 0.0)
        burden_ref[...] = jnp.sum(own, axis=1, keepdims=True) / (rows * width)

    even = at_x % 2 == 0
    above = jnp.where(even, b_ref[...], a_ref[...])
    below = jnp.where(even, a_ref[...], b_ref[...])
    whole = jnp.concatenate([above, mid_ref[...], below], axis=0)
    wide = whole.shape[1]
    down = lax.broadcasted_iota(jnp.int32, whole.shape, 0)
    across = lax.broadcasted_iota(jnp.int32, whole.shape, 1)
    row = at_x * rows + down - rows
    column = at_y * width + jnp.where(across >= width + width // 2, across - wide, across)
    inside = (row >= 0) & (row < count_x * rows) & (column >= 0) & (column < count_y * width)
    keep = jnp.where(inside, relax / 4.0, 0.0)
    whole = jnp.where(inside, whole, 0.0)

    def beside(field, step):
        return (
            pltpu.roll(field, step, 0)
            + pltpu.roll(field, field.shape[0] - step, 0)
            + pltpu.roll(field, step, 1)
            + pltpu.roll(field, wide - step, 1)
        )

    def needed(level, lo, hi):
        step = 2**level
        if level == LEVELS - 1:
            return lo - (COARSE - 1) * step, hi + (COARSE - 1) * step
        lo, hi = needed(level + 1, *coarse_rows(level, lo, hi))
        lo, hi = lo // (2 * step) * (2 * step), round_up(hi, 2 * step)
        return lo - SWEEPS * step, hi + SWEEPS * step

    def coarse_rows(level, lo, hi):
        step = 2**level
        lo, hi = lo - SWEEPS * step, hi + SWEEPS * step
        return lo // (2 * step) * (2 * step), round_up(hi, 2 * step)

    def cut(field, base, lo, hi):
        lo = max(lo // 8 * 8, base)
        hi = min(round_up(hi, 8), base + field.shape[0])
        return field[lo - base : hi - base], lo

    def like(full, field, base):
        return full[base : base + field.shape[0]]

    def halve(field, base, step):
        odd = (like(down, field, base) & step) != 0
        tall = field.shape[0]
        field = field + jnp.where(odd, pltpu.roll(field, step, 0), pltpu.roll(field, tall - step, 0))
        odd = (like(across, field, base) & step) != 0
        field = field + jnp.where(odd, pltpu.roll(field, step, 1), pltpu.roll(field, wide - step, 1))
        return 0.25 * field

    def sweeps(field, source, base, step, count, lo, hi):
        for left in range(count, 0, -1):
            was = base
            field, base = cut(field, was, lo - left * step, hi + left * step)
            source, _ = cut(source, was, lo - left * step, hi + left * step)
            field = like(keep, field, base) * ((field + source) + beside(field, step))
        return field, base

    def vcycle(rhs, base, level, lo, hi):
        step = 2**level
        scale = 4.0**level
        source = scale * rhs
        field = like(keep, rhs, base) * source
        if level == LEVELS - 1:
            return sweeps(field, source, base, step, COARSE - 1, lo, hi)
        for _ in range(SWEEPS - 1):
            field = like(keep, rhs, base) * ((field + source) + beside(field, step))
        resid = rhs - (4.0 * field - beside(field, step)) / scale
        coarse_lo, coarse_hi = coarse_rows(level, lo, hi)
        resid, coarse_base = cut(resid, base, *needed(level + 1, coarse_lo, coarse_hi))
        resid = halve(resid, coarse_base, step)
        coarse, coarse_base = vcycle(resid, coarse_base, level + 1, coarse_lo, coarse_hi)
        coarse, coarse_base = cut(coarse, coarse_base, coarse_lo, coarse_hi)
        part = slice(coarse_base - base, coarse_base - base + coarse.shape[0])
        return sweeps(field[part] + coarse, source[part], coarse_base, step, SWEEPS, lo, hi)

    field, base = vcycle(whole, 0, 0, rows, 2 * rows)
    out_ref[...] = field[rows - base : 2 * rows - base, :width]


def multigrid(mid, a, b, shares, reach, count_x, count_y):
    rows = mid.shape[0]
    width = mid.shape[1] // 2
    quick = shares is not None
    vmem = pl.BlockSpec(memory_space=pltpu.VMEM)
    field = jax.ShapeDtypeStruct((rows, width), f32)
    return pl.pallas_call(
        functools.partial(
            multigrid_kernel, reach=reach, quick=quick, count_x=count_x, count_y=count_y
        ),
        out_shape=(field, jax.ShapeDtypeStruct((1, 1), f32)) if quick else field,
        in_specs=[vmem] * (4 if quick else 3),
        out_specs=(vmem, vmem) if quick else vmem,
        compiler_params=pltpu.CompilerParams(vmem_limit_bytes=8 << 20),
        name="multigrid",
    )(*((mid, a, b, shares) if quick else (mid, a, b)))


def paired(axis, first):
    count = lax.axis_size(axis)
    pairs = []
    for low in range(first, count + first, 2):
        one, other = low % count, (low + 1) % count
        pairs += [(one, other), (other, one)]
    return pairs


def across_chips():
    count_x, count_y = lax.axis_size("gx"), lax.axis_size("gy")
    pairs = []
    for i in range(count_x):
        for low in range(1, count_y - 1, 2):
            one, other = i * count_y + low, i * count_y + low + 1
            pairs += [(one, other), (other, one)]
        for j in (0, count_y - 1):
            pairs.append((i * count_y + j, (i ^ 1) * count_y + j))
    return pairs


def shards(
    chemical_concentration,
    thermal_scaled,
    tentative_flow_spread,
    substep_numbers,
    patch_holder_lookup,
    consumed_weighting,
    molar_coefficient,
    frequency_factor_log,
    arrhenius_energy,
    enthalpy_released,
):
    count_x, count_y = lax.axis_size("gx"), lax.axis_size("gy")
    rows, width = thermal_scaled.shape
    spec_new, temp_new, rhs, shares = chemistry(
        chemical_concentration,
        thermal_scaled,
        tentative_flow_spread,
        substep_numbers,
        patch_holder_lookup,
        consumed_weighting,
        molar_coefficient,
        frequency_factor_log,
        arrhenius_energy,
        enthalpy_released,
    )
    reach = 32
    quick = count_x == 4
    far = None
    if quick:
        far = lax.ppermute(shares, "gx", [(i, i ^ 2) for i in range(4)])
    side_a = lax.ppermute(rhs, "gy", paired("gy", 0))
    side_b = lax.ppermute(rhs, ("gx", "gy"), across_chips())
    band = join_sides(rhs, shares, side_a, side_b, reach)
    band_a = lax.ppermute(band, "gx", paired("gx", 0))
    band_b = lax.ppermute(band, "gx", paired("gx", 1))
    if quick:
        field, burden = multigrid(band, band_a, band_b, far, reach, count_x, count_y)
    else:
        field = multigrid(band, band_a, band_b, None, reach, count_x, count_y)
        burden = lax.psum_scatter(
            shares[0, :count_x], "gx", scatter_dimension=0, tiled=True
        ).reshape(1, 1) / (rows * width)
    return spec_new, temp_new, field, burden


def solution(mesh):
    return jax.shard_map(
        shards,
        mesh=mesh,
        in_specs=(
            P(None, "gx", "gy"),
            P("gx", "gy"),
            P("gx", "gy"),
            P("gx", "gy"),
            P("gx", "gy"),
            P(),
            P(),
            P(),
            P(),
            P(),
        ),
        out_specs=(P(None, "gx", "gy"), P("gx", "gy"), P("gx", "gy"), P("gx", "gy")),
        check_vma=False,
    )
```
